512 devices in a mesh: wide: 64 (over z, y), narrow: 8 (over x, core).
Axes of the slice: x: 4, y: 8, z: 8, core: 2. Of those that a mesh axis runs over, the one named last changes fastest.
Arguments:
- pixel_slabs: bfloat16 [256, 3, 64, 128], P('wide', None, 'narrow'), may hold values from -1 to 1
- conv_in_weight: bfloat16 [3, 3, 96, 9], replicated, may hold values from -0.625 to 0.625
- conv_in_bias: float32 [96], replicated, may hold values from -3 to 3
- norm_gain: float32 [96], replicated, may hold values from 0.5 to 1.5
- conv_weight: bfloat16 [3, 3, 96, 288], replicated, may hold values from -0.125 to 0.125
- conv_bias: float32 [96], replicated, may hold values from -3 to 3
- clip_lengths: int32 [6], replicated, may hold values from 1 to 81, 256 in all
- slab_place: int32 [256], replicated, may hold values from 0 to 255, as said below
- tok_place: int32 [65536], replicated, may hold values from 0 to 65535, as said below
Outputs:
- seq_features: bfloat16 [524288, 384], P(('wide', 'narrow'))
The draws below stay inside these ranges and needn't reach their ends.
Inputs may be any that keep to these rules, and one draw needn't show every extreme that they name: `slab_place`: A permutation. The 4 entries of one aligned block (slabs of one index of wide) name exactly 4 distinct owners (value // 4), each exactly once. `tok_place`: A permutation. The 1024 entries of one aligned block (patch rows of one index of wide) name exactly 32 distinct sequence blocks (value // 1024), exactly 32 entries each.
All inputs are finite; a program needn't handle non-finite values.
Results may differ from the reference program's by a relative error of at most 0.0065.
Values may be sent and summed in bfloat16 or wider, within the bound.
A program may use at most 64 MiB of HBM per device.

```python
import math
import jax
import jax.numpy as jnp
import numpy as np
from jax import lax

CH = 96
PIX = 3
FRAMES_DEV = 4
ROWS_DEV = 8
COLS = 128
FRAMES = 256
ROWS = 64
TOK_DEV = 1024
SEQ = 524288
CLIPS = 6
CLIPMAX = 81
SLAB_PEERS = 4
TOK_PEERS = 32
N_WIDE = 64
N_NARROW = 8


def spread_plan(key, senders, per_device, peers):
    capacity = per_device // peers
    keys = jax.random.split(key, 4)
    arrange = jax.random.permutation(keys[0], senders).astype(jnp.int32)
    inverse = jnp.zeros((senders,), jnp.int32).at[arrange].set(jnp.arange(senders, dtype=jnp.int32))
    offsets = jax.random.permutation(keys[1], senders)[:peers].astype(jnp.int32)
    item_perm = jax.vmap(lambda k: jax.random.permutation(k, per_device))(jax.random.split(keys[2], senders)).astype(jnp.int32)
    slot_perm = jax.vmap(lambda k: jax.random.permutation(k, per_device))(jax.random.split(keys[3], senders)).astype(jnp.int32)
    peer_pick = item_perm // capacity
    owner = arrange[(inverse[:, None] + offsets[peer_pick]) % senders]
    slot_index = jnp.take_along_axis(slot_perm[owner.reshape(-1)], item_perm.reshape(-1, 1), axis=1).reshape(senders, per_device)
    return (owner * per_device + slot_index).reshape(-1).astype(jnp.int32)


def draw_slab_place(key, part):
    return spread_plan(jax.random.fold_in(key, 11), N_WIDE, FRAMES_DEV, SLAB_PEERS)


def draw_tok_place(key, part):
    return spread_plan(jax.random.fold_in(key, 23), N_WIDE, TOK_DEV, TOK_PEERS)


def levels(own_key, extent, pieces, smallest, high):
    def one(dim, shards_of):
        draws = jax.random.uniform(jax.random.fold_in(jax.random.fold_in(own_key, 6), dim), (shards_of,), jnp.float32, smallest / len(pieces), high / len(pieces))
        return jnp.repeat(jnp.exp(draws), extent[dim] // shards_of).reshape((-1,) + (1,) * (len(extent) - dim - 1))

    gain = one(*pieces[0])
    for cut in pieces[1:]:
        gain = gain * one(*cut)
    return gain


def split_up(amount, total, reach, slope):
    loads = [(1 << 20) // math.isqrt(standing ** slope) + 1 for standing in range(2, amount + 1)]
    surplus, holding = total - reach - (amount - 1), [1] * (amount - 1)
    while surplus > 0:
        free = [i for i in range(amount - 1) if holding[i] < reach]
        mass, budget = sum([loads[i] for i in free]), surplus
        for i in free:
            addition = min(reach - holding[i], max(1, budget * loads[i] // mass), surplus)
            holding[i] = holding[i] + addition
            surplus = surplus - addition
    return np.array([reach] + holding)


def ragged_sizes(key, count, total, reach, lean):
    if count == 2:
        one = jax.random.randint(key, (), max(1, total - reach), min(reach, total - 1) + 1)
        return jnp.stack([one, total - one])
    lengths = jnp.asarray(split_up(count, total, reach, lean), jnp.int32)
    couples = (count - 1) // 2
    giver, sink = lengths[1:1 + 2 * couples:2], lengths[2:2 + 2 * couples:2]
    room = jnp.minimum(giver - 1, reach - sink)
    shifted = jax.random.randint(jax.random.fold_in(key, 1), (couples,), 0, 1 << 20) % (room + 1)
    lengths = lengths.at[1:1 + 2 * couples:2].set(giver - shifted).at[2:2 + 2 * couples:2].set(sink + shifted)
    return lengths[jax.random.permutation(jax.random.fold_in(key, 2), count)]


def centred(stream_key, dims, spread, most, kind=jnp.bfloat16):
    values = jax.random.normal(stream_key, dims, jnp.float32) * spread
    return jnp.minimum(jnp.maximum(values, -most), most).astype(kind)


def setup_inputs(seed: int = 0) -> dict:
    streams_of = jax.random.split(jax.random.key(seed), 10)
    pixel_slabs = jnp.clip(jax.random.uniform(streams_of[0], (FRAMES, PIX, ROWS, COLS), jnp.float32, -1.0, 1.0) * levels(streams_of[0], (FRAMES, PIX, ROWS, COLS), ((0, 64), (2, 8)), -0.4, 0.0), -1.0, 1.0).astype(jnp.bfloat16)
    conv_in_weight = centred(streams_of[1], (3, 3, CH, 3 * PIX), (27 * PIX) ** -0.5, 0.625)
    conv_in_bias = centred(streams_of[2], (CH,), 0.5, 3.0, jnp.float32)
    norm_gain = jnp.clip(jax.random.uniform(streams_of[3], (CH,), jnp.float32, 0.5, 1.5), 0.5, 1.5)
    conv_weight = centred(streams_of[4], (3, 3, CH, 3 * CH), (27 * CH) ** -0.5, 0.125)
    conv_bias = centred(streams_of[5], (CH,), 0.5, 3.0, jnp.float32)
    clip_lengths = ragged_sizes(streams_of[6], CLIPS, FRAMES, CLIPMAX, 2).astype(jnp.int32)
    slab_place = draw_slab_place(jax.random.fold_in(streams_of[9], 71), 0)
    tok_place = draw_tok_place(jax.random.fold_in(streams_of[9], 71), 0)
    return dict(pixel_slabs=pixel_slabs, conv_in_weight=conv_in_weight, conv_in_bias=conv_in_bias, norm_gain=norm_gain, conv_weight=conv_weight, conv_bias=conv_bias, clip_lengths=clip_lengths, slab_place=slab_place, tok_place=tok_place)


EPSILON = 1e-06

def tap_valid(clip_lengths, frame_ids):
    starts = jnp.cumsum(clip_lengths) - clip_lengths
    reached = starts[None, :] <= frame_ids[:, None]
    latest = lax.optimization_barrier(jnp.max(jnp.where(reached, starts[None, :], -1), axis=1))
    offsets = jnp.where(frame_ids >= 0, frame_ids - latest, -1)
    reach_back = jnp.array([2, 1, 0], jnp.int32)
    return (offsets[:, None] >= reach_back[None, :]).astype(jnp.float32)

def conv_exact(padded_in, valid_taps, weight, bias_vec):
    frame_count = valid_taps.shape[0]
    row_count = padded_in.shape[2] - 2
    col_count = padded_in.shape[3]
    tap_list = []
    for time_tap in range(3):
        piece = padded_in[time_tap:time_tap + frame_count].astype(jnp.float32)
        tap_list.append(piece * valid_taps[:, time_tap, None, None, None])
    stacked = jnp.concatenate(tap_list, axis=1)
    stacked = jnp.pad(stacked, ((0, 0), (0, 0), (0, 0), (1, 1)))
    running = jnp.zeros((frame_count, weight.shape[2], row_count, col_count), jnp.float32)
    for row_tap in range(3):
        for col_tap in range(3):
            window = stacked[:, :, row_tap:row_tap + row_count, col_tap:col_tap + col_count]
            running = running + jnp.einsum('ok,fkyx->foyx', weight[row_tap, col_tap].astype(jnp.float32), window)
    return running + bias_vec[None, :, None, None]

def norm_silu(hidden, norm_gain):
    values = hidden.astype(jnp.float32)
    mean_square = lax.optimization_barrier(jnp.mean(values * values, axis=1, keepdims=True))
    scaled = values * lax.rsqrt(mean_square + EPSILON) * norm_gain[None, :, None, None]
    return jax.nn.silu(scaled).astype(jnp.bfloat16)

def reference(pixel_slabs, conv_in_weight, conv_in_bias, norm_gain, conv_weight, conv_bias, clip_lengths, slab_place, tok_place):
    video = jnp.zeros_like(pixel_slabs).at[slab_place].set(pixel_slabs)
    padded = jnp.pad(video, ((4, 0), (0, 0), (1, 1), (0, 0)))
    channels = conv_in_bias.shape[0]

    def encode(block):
        start = block * FRAMES_DEV
        pixels = lax.dynamic_slice_in_dim(padded, start, FRAMES_DEV + 4, 0)
        wide_frames = start - 2 + jnp.arange(FRAMES_DEV + 2, dtype=jnp.int32)
        hidden = conv_exact(pixels, tap_valid(clip_lengths, wide_frames), conv_in_weight, conv_in_bias).astype(jnp.bfloat16)
        active = jnp.pad(norm_silu(hidden, norm_gain), ((0, 0), (0, 0), (1, 1), (0, 0)))
        own_frames = start + jnp.arange(FRAMES_DEV, dtype=jnp.int32)
        branch = conv_exact(active, tap_valid(clip_lengths, own_frames), conv_weight, conv_bias)
        summed = hidden[2:].astype(jnp.float32) + branch
        blocks = summed.reshape(FRAMES_DEV, channels, N_NARROW, ROWS_DEV // 2, 2, COLS // 2, 2)
        reordered = jnp.transpose(blocks, (2, 0, 3, 5, 4, 6, 1))
        return reordered.reshape(N_NARROW, TOK_DEV, 4 * channels).astype(jnp.bfloat16)
    encoded = lax.map(encode, jnp.arange(N_WIDE, dtype=jnp.int32))
    places = tok_place.reshape(N_WIDE, TOK_DEV)
    owners = places // TOK_DEV
    slot_of = places % TOK_DEV
    narrow_ids = jnp.arange(N_NARROW, dtype=jnp.int32)[None, :, None]
    target = (owners[:, None, :] * N_NARROW + narrow_ids) * TOK_DEV + slot_of[:, None, :]
    result = jnp.zeros((SEQ, 4 * channels), jnp.bfloat16)
    return result.at[target.reshape(-1)].set(encoded.reshape(-1, 4 * channels))
```

```python
import jax
import jax.numpy as jnp
import numpy as np
from jax import lax
from jax.experimental import pallas as pl
from jax.experimental.pallas import tpu as pltpu
from jax.sharding import PartitionSpec as P

EPSILON = 1e-06
MESH = pl.DeviceIdType.MESH
BF = jnp.bfloat16
F32 = jnp.float32
RING = 8
CH = 96
TOK = 1024
FRAME_ROWS = 72
LEAD = 4
NT = (((1,), (1,)), ((), ()))
NN = (((1,), (0,)), ((), ()))


def placement_tables():
    perm = np.zeros((256, 96), np.float32)
    for row in range(20):
        region, inner = (0, 6 + row) if row < 2 else ((1, row - 2) if row < 10 else ((2, row - 10) if row < 18 else (3, row - 18)))
        for parity in range(2):
            for ch in range(3):
                perm[parity * 128 + row * 6 + parity * 3 + ch, region * 24 + ch * 8 + inner] = 1
    pick = np.zeros((2, 64, 128), np.float32)
    for parity in range(2):
        for pair in range(64):
            pick[parity, pair, 2 * pair + parity] = 1
    return perm, pick


def weight_table():
    table = np.zeros((84, 16 * 384), np.float32)
    for ry in range(4):
        for rx in range(4):
            base = (ry * 4 + rx) * 384
            for ky in range(3):
                for kx in range(3):
                    for kt in range(3):
                        for ch in range(3):
                            row, col = ry + ky, rx + kx
                            lane = (col // 2) * 36 + row * 6 + (col % 2) * 3 + ch
                            table[(ky * 3 + kx) * 9 + kt * 3 + ch, base + kt * 128 + lane] = 1
            for part in range(3):
                table[81 + part, base + 2 * 128 + 108 + part] = 1
    return table


def gather_kernel(
    pix, perm, pick, out, edge, own, s0, r0, s1, r1, local_sem, s2, r2, s3, r3, s4, r4
):
    w = lax.axis_index("wide")
    n = lax.axis_index("narrow")
    z, y = w // RING, w % RING
    x, c = n // 2, n % 2
    sibling = (w, x * 2 + 1 - c)
    near = x + 2 * c - 1
    near_ok = jnp.logical_and(near >= 0, near <= 3)
    major = (z, y)
    minor = (y, z)

    def wide_of(piece, maj, mnr):
        return maj * RING + mnr if piece == 0 else mnr * RING + maj

    def along_minor(piece, d):
        return (wide_of(piece, major[piece], (minor[piece] + d) % RING), n)

    def along_major(piece, d):
        return (wide_of(piece, (major[piece] + d) % RING, minor[piece]), n)

    barrier = pltpu.get_barrier_semaphore()
    pl.semaphore_signal(barrier, inc=1, device_id=sibling, device_id_type=MESH)
    for piece in range(2):
        for d in range(1, RING):
            pl.semaphore_signal(barrier, inc=1, device_id=along_minor(piece, d), device_id_type=MESH)

    for side in (1, 3):
        for core in range(2):
            beside = ((x + side) % 4) * 2 + core
            pl.semaphore_signal(barrier, inc=1, device_id=(w, beside), device_id_type=MESH)
    pl.semaphore_wait(barrier, 19)

    def to_sibling():
        return pltpu.make_async_remote_copy(
            pix.at[pl.ds(2 * (1 - c), 2)], edge.at[0], s0.at[0], r0.at[0], sibling, MESH
        )

    def to_near(core):
        return pltpu.make_async_remote_copy(
            pix.at[pl.ds(2 * core, 2)],
            edge.at[2 - c],
            s0.at[1 + core],
            r0.at[2 - c],
            (w, jnp.clip(near, 0, 3) * 2 + core),
            MESH,
        )

    def arrival(region):
        return pltpu.make_async_remote_copy(
            pix.at[pl.ds(0, 2)], edge.at[region], s0.at[0], r0.at[region], sibling, MESH
        )

    to_sibling().start()

    @pl.when(near_ok)
    def _():
        to_near(0).start()
        to_near(1).start()

    @pl.when(x == 0)
    def _():
        edge[1] = jnp.zeros_like(edge[1])

    @pl.when(x == 3)
    def _():
        edge[2] = jnp.zeros_like(edge[2])

    arrival(0).wait_recv()

    @pl.when(x > 0)
    def _():
        arrival(1).wait_recv()

    @pl.when(x < 3)
    def _():
        arrival(2).wait_recv()

    for piece in range(2):
        mine = pix[2 * c + piece].astype(F32).reshape(24, 128)
        other = edge[0, piece].astype(F32).reshape(24, 128)
        low = edge[1, piece].astype(F32).reshape(24, 128)
        high = edge[2, piece].astype(F32).reshape(24, 128)
        first = jnp.where(c == 0, mine, other)
        second = jnp.where(c == 0, other, mine)
        stack = jnp.concatenate([low, first, second, high], axis=0).astype(BF)
        spread = lax.dot_general(perm[...], stack, NN, preferred_element_type=F32).astype(BF)
        rows = lax.dot_general(pick[0], spread[:128], NT, preferred_element_type=F32)
        rows += lax.dot_general(pick[1], spread[128:], NT, preferred_element_type=F32)
        own[piece] = rows.astype(BF)

    def local(piece):
        return pltpu.make_async_copy(
            own.at[piece], out.at[piece, c, major[piece], minor[piece]], local_sem.at[piece]
        )

    def first_hop(piece, d, slot):
        return pltpu.make_async_remote_copy(
            own.at[piece],
            out.at[piece, c, major[piece], slot],
            s1.at[piece, d],
            r1.at[piece, d],
            along_minor(piece, d),
            MESH,
        )

    order = (1, 7, 2, 6, 3, 5, 4)
    for d in order:
        for piece in range(2):
            first_hop(piece, d, minor[piece]).start()
    for piece in range(2):
        local(piece).start()

    def part(piece, chunk, h):
        return out.at[piece, c, chunk, pl.ds(4 * h, 4)]

    def hop(piece, way, k, h):
        step = 1 - 2 * way
        chunk = (major[piece] - step * (k - 1)) % RING
        ref = part(piece, chunk, h)
        return pltpu.make_async_remote_copy(
            ref, ref, s2.at[piece, way, k - 1, h], r2.at[piece, way, k - 1, h], along_major(piece, step), MESH
        )

    def landed(piece, way, k, h):
        step = 1 - 2 * way
        ref = part(piece, (major[piece] - step * k) % RING, h)
        return pltpu.make_async_remote_copy(
            ref, ref, s2.at[piece, way, k - 1, h], r2.at[piece, way, k - 1, h], along_major(piece, step), MESH
        )

    def share(piece, way, k, h, core):
        step = 1 - 2 * way
        ref = out.at[piece, core, (major[piece] - step * k) % RING, pl.ds(4 * h, 4)]
        return pltpu.make_async_remote_copy(
            ref, ref, s3.at[piece, way, k - 1, h], r3.at[piece, way, k - 1, h], sibling, MESH
        )

    def share_own(piece, core):
        ref = out.at[piece, core, major[piece]]
        return pltpu.make_async_remote_copy(ref, ref, s4.at[piece], r4.at[piece], sibling, MESH)

    for piece in range(2):
        local(piece).wait()
        for d in order:
            first_hop(piece, d, (minor[piece] - d) % RING).wait_recv()
        for i in range(2):
            for way in range(2):
                hop(piece, way, 1, i if way == 0 else 1 - i).start()
        share_own(piece, c).start()

    moves = []
    for k in range(1, 5):
        for i in range(2):
            for piece in range(2):
                for way in range(2):
                    h = i if way == 0 else 1 - i
                    if k < 4 or i == 0:
                        moves.append((piece, way, k, h, k < 3 or (k == 3 and i == 0)))
    for piece, way, k, h, onward in moves:
        landed(piece, way, k, h).wait_recv()
        if onward:
            hop(piece, way, k + 1, h).start()
        share(piece, way, k, h, c).start()

    to_sibling().wait_send()

    @pl.when(near_ok)
    def _():
        to_near(0).wait_send()
        to_near(1).wait_send()

    for piece in range(2):
        for d in order:
            first_hop(piece, d, minor[piece]).wait_send()
        share_own(piece, c).wait_send()
        share_own(piece, 1 - c).wait_recv()
    for piece, way, k, h, onward in moves:
        hop(piece, way, k, h).wait_send()
        share(piece, way, k, h, c).wait_send()
        share(piece, way, k, h, 1 - c).wait_recv()


def gather_tables(pixel_slabs):
    perm, pick = placement_tables()
    dma = pltpu.SemaphoreType.DMA
    vmem = pl.BlockSpec(memory_space=pltpu.VMEM)
    return pl.pallas_call(
        gather_kernel,
        out_shape=jax.ShapeDtypeStruct((2, 2, RING, RING, 64, 128), BF),
        in_specs=[vmem, vmem, vmem],
        out_specs=pl.BlockSpec(memory_space=pl.ANY),
        scratch_shapes=[
            pltpu.VMEM((3, 2, 3, 8, 128), BF),
            pltpu.VMEM((2, 64, 128), BF),
            dma((3,)),
            dma((3,)),
            dma((2, RING)),
            dma((2, RING)),
            dma((2,)),
            dma((2, 2, 4, 2)),
            dma((2, 2, 4, 2)),
            dma((2, 2, 4, 2)),
            dma((2, 2, 4, 2)),
            dma((2,)),
            dma((2,)),
        ],
        compiler_params=pltpu.CompilerParams(collective_id=0, has_side_effects=True),
        name="gather_tables",
    )(pixel_slabs, jnp.asarray(perm, BF), jnp.asarray(pick, BF))


def plan_kernel(tok, out):
    base = lax.axis_index("wide") * TOK
    sub = lax.broadcasted_iota(jnp.int32, (32, 256), 0)
    high_of = (sub % 8) * 4 + sub // 8
    lane = lax.broadcasted_iota(jnp.int32, (1, 256), 1)

    def step(t, total):
        row = tok[pl.ds(t, 1), :] - base
        hit = jnp.broadcast_to(row // 32, (32, 256)) == high_of
        one = jnp.broadcast_to(row % 32, (32, 256)) == sub
        times = jnp.where(hit, t.astype(F32), 0.0)
        inner = jnp.where(hit, jnp.broadcast_to(lane, (32, 256)).astype(F32), 0.0)
        left = jnp.concatenate([times, inner], axis=0).astype(BF)
        right = jnp.where(one, 1.0, 0.0).astype(BF)
        return total + lax.dot_general(left, right, NT, preferred_element_type=F32)

    total = lax.fori_loop(0, 256, step, jnp.zeros((64, 32), F32), unroll=8)
    entry = (total[:32] * 256.0 + total[32:]).astype(jnp.int32)
    out[...] = jnp.concatenate([entry[8 * m : 8 * m + 8] for m in range(4)], axis=1)


def invert_plan(tok_place):
    vmem = pl.BlockSpec(memory_space=pltpu.VMEM)
    return pl.pallas_call(
        plan_kernel,
        out_shape=jax.ShapeDtypeStruct((8, 128), jnp.int32),
        in_specs=[vmem],
        out_specs=vmem,
        name="invert_plan",
    )(tok_place.reshape(256, 256))


TILE = 256


def main_kernel(
    entry_s, slab_s, clip_s, entry_v, table, taps, spread, weight, gain, bias2, out, frames, patches, w1, w2, hid, act
):
    n = lax.axis_index("narrow")
    x, c = n // 2, n % 2

    for pos in range(16):
        w1[pos * CH : (pos + 1) * CH, :] = lax.dot_general(
            taps[...], spread[:, pos * 384 : (pos + 1) * 384], NN, preferred_element_type=F32
        ).astype(BF)
    zero = jnp.zeros((CH, CH), F32)
    for kt in range(3):
        for dy in range(2):
            for dx in range(2):
                blocks = []
                for ry in range(4):
                    for rx in range(4):
                        ky, kx = ry - dy, rx - dx
                        inside = 0 <= ky < 3 and 0 <= kx < 3
                        blocks.append(
                            weight[ky, kx, :, kt * CH : (kt + 1) * CH].astype(F32) if inside else zero
                        )
                row = (dy * 2 + dx) * CH
                w2[kt, row : row + CH, :] = jnp.concatenate(blocks, axis=1).astype(BF)

    frames[0 : LEAD * FRAME_ROWS, :] = jnp.zeros((LEAD * FRAME_ROWS, 128), F32)
    frames[(LEAD + 256) * FRAME_ROWS : (LEAD + 256) * FRAME_ROWS + 8, :] = jnp.zeros((8, 128), F32)

    def fill(i, carry):
        piece, core, maj, mnr = i // 128, (i // 64) % 2, (i // 8) % 8, i % 8
        wide = jnp.where(piece == 0, maj * RING + mnr, mnr * RING + maj)
        frame = slab_s[wide * 4 + core * 2 + piece]
        at = pl.multiple_of((frame + LEAD) * FRAME_ROWS, 8)
        frames[pl.ds(at, 8), :] = jnp.zeros((8, 128), F32)
        frames[pl.ds(at + 8, 64), :] = table[i].astype(F32)
        return carry

    lax.fori_loop(0, 256, fill, 0, unroll=4)

    starts = []
    running = jnp.int32(0)
    for i in range(6):
        starts.append(running)
        running = running + clip_s[i]

    lane = lax.broadcasted_iota(jnp.int32, (5, 128), 1)
    when = lax.broadcasted_iota(jnp.int32, (5, 128), 0)

    def pull(s, carry):
        e = entry_s[s]
        t, j, col = e // 256, (e // 64) % 4, e % 64
        latest = jnp.int32(0)
        for i in range(1, 6):
            latest = jnp.where(starts[i] <= t, starts[i], latest)
        base = t * FRAME_ROWS + 7 + col
        turn = 128 - (4 * c + j) * 12
        left = frames[pl.ds(base, 5, stride=FRAME_ROWS), :]
        mid = frames[pl.ds(base + 1, 5, stride=FRAME_ROWS), :]
        right = frames[pl.ds(base + 2, 5, stride=FRAME_ROWS), :]
        left = pltpu.roll(left, turn % 128, 1)
        mid = pltpu.roll(mid, (turn + 36) % 128, 1)
        right = pltpu.roll(right, (turn + 72) % 128, 1)
        row = jnp.where(lane < 36, left, jnp.where(lane < 72, mid, jnp.where(lane < 108, right, 1.0)))
        row = jnp.where(when >= 4 - (t - latest), row, 0.0)
        patches[pl.ds(s, 5, stride=TOK), :] = row
        return carry

    lax.fori_loop(0, TOK, pull, 0, unroll=8)

    half_gain = gain[...] * 0.5

    def tile(g, carry):
        at = pl.multiple_of(g * TILE, TILE)
        e = entry_v[:, pl.ds(at, TILE)]
        t, j, col = e // 256, (e // 64) % 4, e % 64
        latest = jnp.zeros_like(t)
        for i in range(1, 6):
            latest = jnp.where(starts[i] <= t, starts[i], latest)
        age = t - latest
        row_ok = [
            jnp.logical_not(jnp.logical_and(j == 0, n == 0)),
            None,
            None,
            jnp.logical_not(jnp.logical_and(j == 3, n == 7)),
        ]
        col_ok = [col != 0, None, None, col != 63]
        total = jnp.zeros((4 * CH, TILE), F32) + bias2[...]
        for s in range(3):
            block = jnp.concatenate(
                [patches[pl.ds(pl.multiple_of((s + kt) * TOK + at, TILE), TILE), :].astype(BF) for kt in range(3)],
                axis=1,
            )
            hid[...] = lax.dot_general(w1[...], block, NT, preferred_element_type=F32)
            for ry in range(4):
                for rx in range(4):
                    pos = ry * 4 + rx
                    h = hid[pos * CH : (pos + 1) * CH, :]
                    scale = lax.rsqrt(jnp.sum(h * h, axis=0, keepdims=True) * (1.0 / CH) + EPSILON)
                    ok = age >= 2 - s
                    if row_ok[ry] is not None:
                        ok = jnp.logical_and(ok, row_ok[ry])
                    if col_ok[rx] is not None:
                        ok = jnp.logical_and(ok, col_ok[rx])
                    u = h * jnp.where(ok, scale, 0.0) * half_gain
                    act[pos * CH : (pos + 1) * CH, :] = (u + u * jnp.tanh(u)).astype(BF)
            total = total + lax.dot_general(w2[s], act[...], NN, preferred_element_type=F32)
            if s == 2:
                keep = [hid[(ry * 4 + rx) * CH : (ry * 4 + rx + 1) * CH, :] for ry in (1, 2) for rx in (1, 2)]
                total = total + jnp.concatenate(keep, axis=0)
        out[pl.ds(at, TILE), :] = jnp.transpose(total).astype(BF)
        return carry

    lax.fori_loop(0, TOK // TILE, tile, 0)


def encode(entry, slab_place, clip_lengths, table, taps, weight, gain, bias2):
    vmem = pl.BlockSpec(memory_space=pltpu.VMEM)
    smem = pl.BlockSpec(memory_space=pltpu.SMEM)
    return pl.pallas_call(
        main_kernel,
        out_shape=jax.ShapeDtypeStruct((TOK, 4 * CH), BF),
        in_specs=[smem, smem, smem] + [vmem] * 7,
        out_specs=vmem,
        scratch_shapes=[
            pltpu.VMEM(((LEAD + 256) * FRAME_ROWS + 8, 128), F32),
            pltpu.VMEM((5 * TOK, 128), F32),
            pltpu.VMEM((16 * CH, 384), BF),
            pltpu.VMEM((3, 4 * CH, 16 * CH), BF),
            pltpu.VMEM((16 * CH, TILE), F32),
            pltpu.VMEM((16 * CH, TILE), BF),
        ],
        compiler_params=pltpu.CompilerParams(vmem_limit_bytes=56 << 20),
        name="encode",
    )(
        entry.reshape(TOK),
        slab_place,
        clip_lengths,
        entry.reshape(1, TOK),
        table,
        taps,
        jnp.asarray(weight_table(), BF),
        weight,
        gain.reshape(CH, 1),
        bias2.reshape(4 * CH, 1),
    )


def split_bias(bias):
    first = lax.reduce_precision(bias, 8, 7)
    second = lax.reduce_precision(bias - first, 8, 7)
    third = bias - first - second
    return jnp.stack([first, second, third], axis=1).astype(BF)


def body(
    pixel_slabs,
    conv_in_weight,
    conv_in_bias,
    norm_gain,
    conv_weight,
    conv_bias,
    clip_lengths,
    slab_place,
    tok_place,
):
    table = gather_tables(pixel_slabs)
    entry = invert_plan(tok_place)
    taps = jnp.transpose(conv_in_weight, (2, 0, 1, 3)).reshape(CH, 81)
    taps = jnp.concatenate([taps, split_bias(conv_in_bias)], axis=1)
    return encode(
        entry,
        slab_place,
        clip_lengths,
        table.reshape(256, 64, 128),
        taps,
        conv_weight,
        norm_gain,
        jnp.tile(conv_bias, 4),
    )


def solution(mesh):
    placed = (P("wide", None, "narrow", None), P(), P(), P(), P(), P(), P(), P(), P())
    return jax.shard_map(
        body, mesh=mesh, in_specs=placed, out_specs=P(("wide", "narrow"), None), check_vma=False
    )
```

```python
import jax
import jax.numpy as jnp
import numpy as np
from jax import lax
from jax.experimental import pallas as pl
from jax.experimental.pallas import tpu as pltpu
from jax.sharding import PartitionSpec as P

EPSILON = 1e-06
MESH = pl.DeviceIdType.MESH
BF = jnp.bfloat16
F32 = jnp.float32
RING = 8
CH = 96
TOK = 1024
FRAME_ROWS = 72
LEAD = 4
NT = (((1,), (1,)), ((), ()))
NN = (((1,), (0,)), ((), ()))


def placement_tables():
    perm = np.zeros((256, 96), np.float32)
    for row in range(20):
        region, inner = (0, 6 + row) if row < 2 else ((1, row - 2) if row < 10 else ((2, row - 10) if row < 18 else (3, row - 18)))
        for parity in range(2):
            for ch in range(3):
                perm[parity * 128 + row * 6 + parity * 3 + ch, region * 24 + ch * 8 + inner] = 1
    pick = np.zeros((2, 64, 128), np.float32)
    for parity in range(2):
        for pair in range(64):
            pick[parity, pair, 2 * pair + parity] = 1
    return perm, pick


def weight_table():
    table = np.zeros((2, 84, 16 * 384), np.float32)
    for core in range(2):
        for ry in range(4):
            for rx in range(4):
                base = (ry * 4 + rx) * 384
                for ky in range(3):
                    for kx in range(3):
                        for kt in range(3):
                            for ch in range(3):
                                row, col = ry + ky, rx + kx
                                lane = (col // 2) * 36 + row * 6 + (col % 2) * 3 + ch
                                lane = (lane + 48 * core) % 128
                                table[core, (ky * 3 + kx) * 9 + kt * 3 + ch, base + kt * 128 + lane] = 1
                for part in range(3):
                    table[core, 81 + part, base + 2 * 128 + (108 + part + 48 * core) % 128] = 1
    return table


def gather_kernel(
    pix, perm, pick, out, edge, own, s0, r0, s1, r1, local_sem, s2, r2, s3, r3, s4, r4
):
    w = lax.axis_index("wide")
    n = lax.axis_index("narrow")
    z, y = w // RING, w % RING
    x, c = n // 2, n % 2
    sibling = (w, x * 2 + 1 - c)
    near = x + 2 * c - 1
    near_ok = jnp.logical_and(near >= 0, near <= 3)
    major = (z, y)
    minor = (y, z)

    def wide_of(piece, maj, mnr):
        return maj * RING + mnr if piece == 0 else mnr * RING + maj

    def along_minor(piece, d):
        return (wide_of(piece, major[piece], (minor[piece] + d) % RING), n)

    def along_major(piece, d):
        return (wide_of(piece, (major[piece] + d) % RING, minor[piece]), n)

    barrier = pltpu.get_barrier_semaphore()
    pl.semaphore_signal(barrier, inc=1, device_id=sibling, device_id_type=MESH)
    for piece in range(2):
        for d in range(1, RING):
            pl.semaphore_signal(barrier, inc=1, device_id=along_minor(piece, d), device_id_type=MESH)

    for side in (1, 3):
        for core in range(2):
            beside = ((x + side) % 4) * 2 + core
            pl.semaphore_signal(barrier, inc=1, device_id=(w, beside), device_id_type=MESH)
    pl.semaphore_wait(barrier, 19)

    def to_sibling():
        return pltpu.make_async_remote_copy(
            pix.at[pl.ds(2 * (1 - c), 2)], edge.at[0], s0.at[0], r0.at[0], sibling, MESH
        )

    def to_near(core):
        return pltpu.make_async_remote_copy(
            pix.at[pl.ds(2 * core, 2)],
            edge.at[2 - c],
            s0.at[1 + core],
            r0.at[2 - c],
            (w, jnp.clip(near, 0, 3) * 2 + core),
            MESH,
        )

    def arrival(region):
        return pltpu.make_async_remote_copy(
            pix.at[pl.ds(0, 2)], edge.at[region], s0.at[0], r0.at[region], sibling, MESH
        )

    to_sibling().start()

    @pl.when(near_ok)
    def _():
        to_near(0).start()
        to_near(1).start()

    @pl.when(x == 0)
    def _():
        edge[1] = jnp.zeros_like(edge[1])

    @pl.when(x == 3)
    def _():
        edge[2] = jnp.zeros_like(edge[2])

    arrival(0).wait_recv()

    @pl.when(x > 0)
    def _():
        arrival(1).wait_recv()

    @pl.when(x < 3)
    def _():
        arrival(2).wait_recv()

    for piece in range(2):
        mine = pix[2 * c + piece].astype(F32).reshape(24, 128)
        other = edge[0, piece].astype(F32).reshape(24, 128)
        low = edge[1, piece].astype(F32).reshape(24, 128)
        high = edge[2, piece].astype(F32).reshape(24, 128)
        first = jnp.where(c == 0, mine, other)
        second = jnp.where(c == 0, other, mine)
        stack = jnp.concatenate([low, first, second, high], axis=0).astype(BF)
        spread = lax.dot_general(perm[...], stack, NN, preferred_element_type=F32).astype(BF)
        rows = lax.dot_general(pick[0], spread[:128], NT, preferred_element_type=F32)
        rows += lax.dot_general(pick[1], spread[128:], NT, preferred_element_type=F32)
        own[piece] = rows.astype(BF)

    def local(piece):
        return pltpu.make_async_copy(
            own.at[piece], out.at[piece, c, major[piece], minor[piece]], local_sem.at[piece]
        )

    def first_hop(piece, d, slot):
        return pltpu.make_async_remote_copy(
            own.at[piece],
            out.at[piece, c, major[piece], slot],
            s1.at[piece, d],
            r1.at[piece, d],
            along_minor(piece, d),
            MESH,
        )

    order = (1, 7, 2, 6, 3, 5, 4)
    for d in order:
        for piece in range(2):
            first_hop(piece, d, minor[piece]).start()
    for piece in range(2):
        local(piece).start()

    def part(piece, chunk, h):
        return out.at[piece, c, chunk, pl.ds(4 * h, 4)]

    def hop(piece, way, k, h):
        step = 1 - 2 * way
        chunk = (major[piece] - step * (k - 1)) % RING
        ref = part(piece, chunk, h)
        return pltpu.make_async_remote_copy(
            ref, ref, s2.at[piece, way, k - 1, h], r2.at[piece, way, k - 1, h], along_major(piece, step), MESH
        )

    def landed(piece, way, k, h):
        step = 1 - 2 * way
        ref = part(piece, (major[piece] - step * k) % RING, h)
        return pltpu.make_async_remote_copy(
            ref, ref, s2.at[piece, way, k - 1, h], r2.at[piece, way, k - 1, h], along_major(piece, step), MESH
        )

    def share(piece, way, k, h, core):
        step = 1 - 2 * way
        ref = out.at[piece, core, (major[piece] - step * k) % RING, pl.ds(4 * h, 4)]
        return pltpu.make_async_remote_copy(
            ref, ref, s3.at[piece, way, k - 1, h], r3.at[piece, way, k - 1, h], sibling, MESH
        )

    def share_own(piece, core):
        ref = out.at[piece, core, major[piece]]
        return pltpu.make_async_remote_copy(ref, ref, s4.at[piece], r4.at[piece], sibling, MESH)

    for piece in range(2):
        local(piece).wait()
        for d in order:
            first_hop(piece, d, (minor[piece] - d) % RING).wait_recv()
        for i in range(2):
            for way in range(2):
                hop(piece, way, 1, i if way == 0 else 1 - i).start()
        share_own(piece, c).start()

    moves = []
    for k in range(1, 5):
        for i in range(2):
            for piece in range(2):
                for way in range(2):
                    h = i if way == 0 else 1 - i
                    if k < 4 or i == 0:
                        moves.append((piece, way, k, h, k < 3 or (k == 3 and i == 0)))
    for piece, way, k, h, onward in moves:
        landed(piece, way, k, h).wait_recv()
        if onward:
            hop(piece, way, k + 1, h).start()
        share(piece, way, k, h, c).start()

    to_sibling().wait_send()

    @pl.when(near_ok)
    def _():
        to_near(0).wait_send()
        to_near(1).wait_send()

    for piece in range(2):
        for d in order:
            first_hop(piece, d, minor[piece]).wait_send()
        share_own(piece, c).wait_send()
        share_own(piece, 1 - c).wait_recv()
    for piece, way, k, h, onward in moves:
        hop(piece, way, k, h).wait_send()
        share(piece, way, k, h, c).wait_send()
        share(piece, way, k, h, 1 - c).wait_recv()


def gather_tables(pixel_slabs):
    perm, pick = placement_tables()
    dma = pltpu.SemaphoreType.DMA
    vmem = pl.BlockSpec(memory_space=pltpu.VMEM)
    return pl.pallas_call(
        gather_kernel,
        out_shape=jax.ShapeDtypeStruct((2, 2, RING, RING, 64, 128), BF),
        in_specs=[vmem, vmem, vmem],
        out_specs=pl.BlockSpec(memory_space=pl.ANY),
        scratch_shapes=[
            pltpu.VMEM((3, 2, 3, 8, 128), BF),
            pltpu.VMEM((2, 64, 128), BF),
            dma((3,)),
            dma((3,)),
            dma((2, RING)),
            dma((2, RING)),
            dma((2,)),
            dma((2, 2, 4, 2)),
            dma((2, 2, 4, 2)),
            dma((2, 2, 4, 2)),
            dma((2, 2, 4, 2)),
            dma((2,)),
            dma((2,)),
        ],
        compiler_params=pltpu.CompilerParams(collective_id=0, has_side_effects=True),
        name="gather_tables",
    )(pixel_slabs, jnp.asarray(perm, BF), jnp.asarray(pick, BF))


def clip_age(starts, t):
    latest = jnp.zeros_like(t)
    for i in range(1, 6):
        latest = jnp.where(starts[i] <= t, starts[i], latest)
    return t - latest


def clip_starts(clip_s):
    starts = [jnp.int32(0)]
    for i in range(5):
        starts.append(starts[-1] + clip_s[i])
    return starts


def plan_kernel(clip_s, tok, words, entry):
    base = lax.axis_index("wide") * TOK
    sub = lax.broadcasted_iota(jnp.int32, (32, 256), 0)
    high_of = (sub % 8) * 4 + sub // 8
    inside = lax.broadcasted_iota(jnp.int32, (32, 256), 1).astype(F32)

    def step(t, total):
        pair = [jnp.broadcast_to(tok[pl.ds(2 * t + i, 1), :] - base, (32, 128)) for i in range(2)]
        row = jnp.concatenate(pair, axis=1)
        hit = row >> 5 == high_of
        times = jnp.where(hit, t.astype(F32), 0.0)
        inner = jnp.where(hit, inside, 0.0)
        left = jnp.concatenate([times, inner], axis=0).astype(BF)
        right = jnp.where(row & 31 == sub, 1.0, 0.0).astype(BF)
        return total + lax.dot_general(left, right, NT, preferred_element_type=F32)

    total = lax.fori_loop(0, 256, step, jnp.zeros((64, 32), F32), unroll=8)
    found = (total[:32] * 256.0 + total[32:]).astype(jnp.int32)
    e = jnp.concatenate([found[8 * m : 8 * m + 8] for m in range(4)], axis=1)
    entry[...] = e
    t, j, col = e >> 8, (e >> 6) & 3, e & 63
    words[0:8, :] = t * FRAME_ROWS + 7 + col
    words[8:16, :] = j
    words[16:24, :] = 4 - clip_age(clip_starts(clip_s), t)


def invert_plan(clip_lengths, tok_place):
    vmem = pl.BlockSpec(memory_space=pltpu.VMEM)
    smem = pl.BlockSpec(memory_space=pltpu.SMEM)
    return pl.pallas_call(
        plan_kernel,
        out_shape=(jax.ShapeDtypeStruct((24, 128), jnp.int32), jax.ShapeDtypeStruct((8, 128), jnp.int32)),
        in_specs=[smem, vmem],
        out_specs=(vmem, vmem),
        name="invert_plan",
    )(clip_lengths, tok_place.reshape(512, 128))


TILE = 256
BATCH = 8


def column(row):
    n = row.shape[1]
    same = lax.broadcasted_iota(jnp.int32, (n, n), 0) == lax.broadcasted_iota(jnp.int32, (n, n), 1)
    return jnp.sum(jnp.where(same, jnp.broadcast_to(row, (n, n)), 0.0), axis=1, keepdims=True)


def main_kernel(
    words,
    slab_s,
    clip_s,
    entry,
    table,
    spread_all,
    in_weight,
    in_bias,
    gain,
    weight,
    bias,
    out,
    held,
    spread,
    frames,
    patches,
    shifts,
    w1,
    w2,
    hid,
    act,
    load_sem,
    spread_sem,
):
    n = lax.axis_index("narrow")
    c = n % 2

    def load(k):
        return pltpu.make_async_copy(table.at[pl.ds(32 * k, 32)], held.at[pl.ds(32 * k, 32)], load_sem.at[k])

    fetch = pltpu.make_async_copy(spread_all.at[c], spread, spread_sem)
    for k in range(8):
        load(k).start()
        if k == 0:
            fetch.start()

    zero = jnp.zeros((CH, CH), F32)
    for kt in range(3):
        for dy in range(2):
            for dx in range(2):
                blocks = []
                for ry in range(4):
                    for rx in range(4):
                        ky, kx = ry - dy, rx - dx
                        within = 0 <= ky < 3 and 0 <= kx < 3
                        blocks.append(
                            weight[ky, kx, :, kt * CH : (kt + 1) * CH].astype(F32) if within else zero
                        )
                row = (dy * 2 + dx) * CH
                w2[kt, row : row + CH, :] = jnp.concatenate(blocks, axis=1).astype(BF)

    half_gain = column(gain[...]) * 0.5
    out_bias = column(bias[...])
    first = column(in_bias[...])
    split = []
    for _ in range(3):
        part = first.astype(BF).astype(F32)
        split.append(part)
        first = first - part
    taps = [in_weight[ky, kx].astype(F32) for ky in range(3) for kx in range(3)]
    taps = jnp.concatenate(taps + split, axis=1).astype(BF)
    lane = lax.broadcasted_iota(jnp.int32, (8, 128), 1)
    for j in range(4):
        shifts[8 * j : 8 * j + 8, :] = (lane + 256 - (48 * c + 12 * j)) & 127
    fetch.wait()
    for pos in range(16):
        w1[pos * CH : (pos + 1) * CH, :] = lax.dot_general(
            taps, spread[:, pos * 384 : (pos + 1) * 384], NN, preferred_element_type=F32
        ).astype(BF)

    frames[0 : LEAD * FRAME_ROWS, :] = jnp.zeros((LEAD * FRAME_ROWS, 128), F32)
    frames[(LEAD + 256) * FRAME_ROWS : (LEAD + 256) * FRAME_ROWS + 8, :] = jnp.zeros((8, 128), F32)
    for k in range(8):
        piece, core = k // 4, (k // 2) % 2
        load(k).wait()

        def fill(m, carry):
            maj = (k % 2) * 4 + m
            at = []
            for mnr in range(RING):
                wide = maj * RING + mnr if piece == 0 else mnr * RING + maj
                frame = slab_s[wide * 4 + core * 2 + piece]
                at.append(pl.multiple_of((frame + LEAD) * FRAME_ROWS, 8))
            for mnr in range(RING):
                frames[pl.ds(at[mnr], 8), :] = jnp.zeros((8, 128), F32)
                frames[pl.ds(at[mnr] + 8, 64), :] = held[32 * k + m * RING + mnr].astype(F32)
            return carry

        lax.fori_loop(0, 4, fill, 0)

    late = lax.broadcasted_iota(jnp.int32, (5, 128), 0)

    def pick_up(s):
        base, j, least = words[s], words[TOK + s], words[2 * TOK + s]
        rel = shifts[pl.ds(pl.multiple_of(j * 8, 8), 5), :]
        left = frames[pl.ds(base, 5, stride=FRAME_ROWS), :]
        mid = pltpu.roll(frames[pl.ds(base + 1, 5, stride=FRAME_ROWS), :], 36, 1)
        right = pltpu.roll(frames[pl.ds(base + 2, 5, stride=FRAME_ROWS), :], 72, 1)
        row = jnp.where(rel < 36, left, jnp.where(rel < 72, mid, jnp.where(rel < 108, right, 1.0)))
        row = jnp.where(late >= least, row, 0.0)
        return pltpu.roll(row, 128 - 12 * j, 1)

    def pull(q, carry):
        rows = [pick_up(q * BATCH + i) for i in range(BATCH)]
        for i in range(BATCH):
            patches[pl.ds(q * BATCH + i, 5, stride=TOK), :] = rows[i]
        return carry

    lax.fori_loop(0, TOK // BATCH, pull, 0)

    starts = clip_starts(clip_s)

    def tile(g, carry):
        at = pl.multiple_of(g * TILE, TILE)
        e = jnp.concatenate([entry[pl.ds(g * (TILE // 128) + i, 1), :] for i in range(TILE // 128)], axis=1)
        t, j, col = e >> 8, (e >> 6) & 3, e & 63
        age = clip_age(starts, t)
        row_ok = [
            jnp.logical_not(jnp.logical_and(j == 0, n == 0)),
            None,
            None,
            jnp.logical_not(jnp.logical_and(j == 3, n == 7)),
        ]
        col_ok = [col != 0, None, None, col != 63]
        total = jnp.concatenate([jnp.broadcast_to(out_bias, (CH, TILE))] * 4, axis=0)
        for s in range(3):
            block = jnp.concatenate(
                [patches[pl.ds(pl.multiple_of((s + kt) * TOK + at, TILE), TILE), :].astype(BF) for kt in range(3)],
                axis=1,
            )
            hid[...] = lax.dot_general(w1[...], block, NT, preferred_element_type=F32)
            for ry in range(4):
                for rx in range(4):
                    pos = ry * 4 + rx
                    h = hid[pos * CH : (pos + 1) * CH, :]
                    scale = lax.rsqrt(jnp.sum(h * h, axis=0, keepdims=True) * (1.0 / CH) + EPSILON)
                    ok = age >= 2 - s
                    if row_ok[ry] is not None:
                        ok = jnp.logical_and(ok, row_ok[ry])
                    if col_ok[rx] is not None:
                        ok = jnp.logical_and(ok, col_ok[rx])
                    u = h * jnp.where(ok, scale, 0.0) * half_gain
                    act[pos * CH : (pos + 1) * CH, :] = (u + u * jnp.tanh(u)).astype(BF)
            total = total + lax.dot_general(w2[s], act[...], NN, preferred_element_type=F32)
            if s == 2:
                keep = [hid[(ry * 4 + rx) * CH : (ry * 4 + rx + 1) * CH, :] for ry in (1, 2) for rx in (1, 2)]
                total = total + jnp.concatenate(keep, axis=0)
        out[pl.ds(at, TILE), :] = jnp.transpose(total).astype(BF)
        return carry

    lax.fori_loop(0, TOK // TILE, tile, 0)


def encode(words, entry, slab_place, clip_lengths, table, in_weight, in_bias, gain, weight, bias):
    vmem = pl.BlockSpec(memory_space=pltpu.VMEM)
    smem = pl.BlockSpec(memory_space=pltpu.SMEM)
    anywhere = pl.BlockSpec(memory_space=pl.ANY)
    return pl.pallas_call(
        main_kernel,
        out_shape=jax.ShapeDtypeStruct((TOK, 4 * CH), BF),
        in_specs=[smem, smem, smem, vmem, anywhere, anywhere] + [vmem] * 5,
        out_specs=vmem,
        scratch_shapes=[
            pltpu.VMEM((256, 64, 128), BF),
            pltpu.VMEM((84, 16 * 384), BF),
            pltpu.VMEM(((LEAD + 256) * FRAME_ROWS + 8, 128), F32),
            pltpu.VMEM((5 * TOK, 128), F32),
            pltpu.VMEM((32, 128), jnp.int32),
            pltpu.VMEM((16 * CH, 384), BF),
            pltpu.VMEM((3, 4 * CH, 16 * CH), BF),
            pltpu.VMEM((16 * CH, TILE), F32),
            pltpu.VMEM((16 * CH, TILE), BF),
            pltpu.SemaphoreType.DMA((8,)),
            pltpu.SemaphoreType.DMA,
        ],
        compiler_params=pltpu.CompilerParams(vmem_limit_bytes=56 << 20),
        name="encode",
    )(
        words.reshape(3 * TOK),
        slab_place,
        clip_lengths,
        entry,
        table,
        jnp.asarray(weight_table(), BF),
        in_weight,
        in_bias.reshape(1, CH),
        gain.reshape(1, CH),
        weight,
        bias.reshape(1, CH),
    )


def body(
    pixel_slabs,
    conv_in_weight,
    conv_in_bias,
    norm_gain,
    conv_weight,
    conv_bias,
    clip_lengths,
    slab_place,
    tok_place,
):
    table = gather_tables(pixel_slabs)
    words, entry = invert_plan(clip_lengths, tok_place)
    return encode(
        words,
        entry,
        slab_place,
        clip_lengths,
        table.reshape(256, 64, 128),
        conv_in_weight,
        conv_in_bias,
        norm_gain,
        conv_weight,
        conv_bias,
    )


def solution(mesh):
    placed = (P("wide", None, "narrow", None), P(), P(), P(), P(), P(), P(), P(), P())
    return jax.shard_map(
        body, mesh=mesh, in_specs=placed, out_specs=P(("wide", "narrow"), None), check_vma=False
    )
```

```python
import jax
import jax.numpy as jnp
import numpy as np
from jax import lax
from jax.experimental import pallas as pl
from jax.experimental.pallas import tpu as pltpu
from jax.sharding import PartitionSpec as P

EPSILON = 1e-06
MESH = pl.DeviceIdType.MESH
BF = jnp.bfloat16
F32 = jnp.float32
RING = 8
CH = 96
TOK = 1024
FRAME_ROWS = 72
LEAD = 4
NT = (((1,), (1,)), ((), ()))
NN = (((1,), (0,)), ((), ()))


def placement_tables():
    perm = np.zeros((256, 96), np.float32)
    for row in range(20):
        region, inner = (0, 6 + row) if row < 2 else ((1, row - 2) if row < 10 else ((2, row - 10) if row < 18 else (3, row - 18)))
        for parity in range(2):
            for ch in range(3):
                perm[parity * 128 + row * 6 + parity * 3 + ch, region * 24 + ch * 8 + inner] = 1
    pick = np.zeros((2, 64, 128), np.float32)
    for parity in range(2):
        for pair in range(64):
            pick[parity, pair, 2 * pair + parity] = 1
    return perm, pick


def weight_table():
    table = np.zeros((2, 84, 16 * 384), np.float32)
    for core in range(2):
        for ry in range(4):
            for rx in range(4):
                base = (ry * 4 + rx) * 384
                for ky in range(3):
                    for kx in range(3):
                        for kt in range(3):
                            for ch in range(3):
                                row, col = ry + ky, rx + kx
                                lane = (col // 2) * 36 + row * 6 + (col % 2) * 3 + ch
                                lane = (lane + 48 * core) % 128
                                table[core, (ky * 9 + kt * 3 + ch) * 3 + kx, base + kt * 128 + lane] = 1
                for part in range(3):
                    table[core, 81 + part, base + 2 * 128 + (108 + part + 48 * core) % 128] = 1
    return table


def clip_age(starts, t):
    latest = jnp.zeros_like(t)
    for i in range(1, 6):
        latest = jnp.where(starts[i] <= t, starts[i], latest)
    return t - latest


def clip_starts(clip_s):
    starts = [jnp.int32(0)]
    for i in range(5):
        starts.append(starts[-1] + clip_s[i])
    return starts


PLAN = 1024


def plan_steps(tok, total, base, first, last):
    sub = lax.broadcasted_iota(jnp.int32, (32, PLAN), 0)
    high_of = (sub % 8) * 4 + sub // 8
    lane = lax.broadcasted_iota(jnp.int32, (32, PLAN), 1)
    inside = (lane % 256).astype(F32)
    frame = (lane // 256).astype(F32)

    def step(q, carry):
        rows = tok[pl.ds(pl.multiple_of(q * 8, 8), 8), :] - base
        row = jnp.concatenate([jnp.broadcast_to(rows[i : i + 1], (32, 128)) for i in range(8)], axis=1)
        hit = row >> 5 == high_of
        times = jnp.where(hit, frame + (q * (PLAN // 256)).astype(F32), 0.0)
        inner = jnp.where(hit, inside, 0.0)
        left = jnp.concatenate([times, inner], axis=0).astype(BF)
        right = jnp.where(row & 31 == sub, 1.0, 0.0).astype(BF)
        total[...] += lax.dot_general(left, right, NT, preferred_element_type=F32)
        return carry

    lax.fori_loop(first, last, step, 0)


def plan_words(total, starts, words, entry):
    found = (total[:32, :] * 256.0 + total[32:, :]).astype(jnp.int32)
    e = jnp.concatenate([found[8 * m : 8 * m + 8] for m in range(4)], axis=1)
    entry[...] = e
    t, j, col = e >> 8, (e >> 6) & 3, e & 63
    words[0:8, :] = t * FRAME_ROWS + 7 + col
    words[8:16, :] = j
    words[16:24, :] = 4 - clip_age(starts, t)


SUBS = 2


def gather_kernel(
    clip_s, pix, tok, perm, pick, out, words, entry, own, edge, total, s0, r0, s1, r1, keep, s2, r2, s3, r3, s4, r4
):
    w = lax.axis_index("wide")
    n = lax.axis_index("narrow")
    z, y = w // RING, w % RING
    x, c = n // 2, n % 2
    sibling = (w, x * 2 + 1 - c)
    near = x + 2 * c - 1
    near_ok = jnp.logical_and(near >= 0, near <= 3)
    major = (z, y)
    minor = (y, z)

    def wide_of(piece, maj, mnr):
        return maj * RING + mnr if piece == 0 else mnr * RING + maj

    def along_minor(piece, d):
        return (wide_of(piece, major[piece], (minor[piece] + d) % RING), n)

    def along_major(piece, d):
        return (wide_of(piece, (major[piece] + d) % RING, minor[piece]), n)

    barrier = pltpu.get_barrier_semaphore()
    pl.semaphore_signal(barrier, inc=1, device_id=sibling, device_id_type=MESH)
    for piece in range(2):
        for d in range(1, RING):
            pl.semaphore_signal(barrier, inc=1, device_id=along_minor(piece, d), device_id_type=MESH)

    for side in (1, 3):
        for core in range(2):
            beside = ((x + side) % 4) * 2 + core
            pl.semaphore_signal(barrier, inc=1, device_id=(w, beside), device_id_type=MESH)
    pl.semaphore_wait(barrier, 19)

    def to_sibling():
        return pltpu.make_async_remote_copy(
            pix.at[pl.ds(2 * (1 - c), 2)], edge.at[0], s0.at[0], r0.at[0], sibling, MESH
        )

    def to_near(core):
        return pltpu.make_async_remote_copy(
            pix.at[pl.ds(2 * core, 2)],
            edge.at[2 - c],
            s0.at[1 + core],
            r0.at[2 - c],
            (w, jnp.clip(near, 0, 3) * 2 + core),
            MESH,
        )

    def arrival(region):
        return pltpu.make_async_remote_copy(
            pix.at[pl.ds(0, 2)], edge.at[region], s0.at[0], r0.at[region], sibling, MESH
        )

    to_sibling().start()

    @pl.when(near_ok)
    def _():
        to_near(0).start()
        to_near(1).start()

    @pl.when(x == 0)
    def _():
        edge[1] = jnp.zeros_like(edge[1])

    @pl.when(x == 3)
    def _():
        edge[2] = jnp.zeros_like(edge[2])

    arrival(0).wait_recv()

    @pl.when(x > 0)
    def _():
        arrival(1).wait_recv()

    @pl.when(x < 3)
    def _():
        arrival(2).wait_recv()

    for piece in range(2):
        mine = pix[2 * c + piece].astype(F32).reshape(24, 128)
        other = edge[0, piece].astype(F32).reshape(24, 128)
        low = edge[1, piece].astype(F32).reshape(24, 128)
        high = edge[2, piece].astype(F32).reshape(24, 128)
        first = jnp.where(c == 0, mine, other)
        second = jnp.where(c == 0, other, mine)
        stack = jnp.concatenate([low, first, second, high], axis=0).astype(BF)
        spread = lax.dot_general(perm[...], stack, NN, preferred_element_type=F32).astype(BF)
        rows = lax.dot_general(pick[0], spread[:128], NT, preferred_element_type=F32)
        rows += lax.dot_general(pick[1], spread[128:], NT, preferred_element_type=F32)
        own[piece] = rows.astype(BF)

    def local(piece):
        return pltpu.make_async_copy(own.at[piece], out.at[piece, c, major[piece], minor[piece]], keep.at[piece])

    def first_hop(piece, d, slot):
        return pltpu.make_async_remote_copy(
            own.at[piece],
            out.at[piece, c, major[piece], slot],
            s1.at[piece, d],
            r1.at[piece, d],
            along_minor(piece, d),
            MESH,
        )

    order = (4, 3, 5, 2, 6, 1, 7)
    for piece in range(2):
        for d in order:
            first_hop(piece, d, minor[piece]).start()
    for piece in range(2):
        local(piece).start()

    total[...] = jnp.zeros_like(total)
    plan_steps(tok, total, w * TOK, 0, PLAN_A)

    part = RING // SUBS

    def hop(piece, way, k, h, arrived):
        step = 1 - 2 * way
        chunk = (major[piece] - step * (k if arrived else k - 1)) % RING
        ref = out.at[piece, c, chunk, pl.ds(part * h, part)]
        return pltpu.make_async_remote_copy(
            ref, ref, s2.at[piece, way, k - 1, h], r2.at[piece, way, k - 1, h], along_major(piece, step), MESH
        )

    def share(piece, way, k, h, core):
        chunk = (major[piece] - (1 - 2 * way) * k) % RING
        where = (piece, core, chunk, pl.ds(part * h, part))
        return pltpu.make_async_remote_copy(
            out.at[where], out.at[where], s3.at[piece, way, k - 1, h], r3.at[piece, way, k - 1, h], sibling, MESH
        )

    def share_own(piece, core):
        where = (piece, core, major[piece])
        return pltpu.make_async_remote_copy(out.at[where], out.at[where], s4.at[piece], r4.at[piece], sibling, MESH)

    def turned(way, i):
        return i if way == 0 else SUBS - 1 - i

    for piece in range(2):
        local(piece).wait()
        for d in reversed(order):
            first_hop(piece, d, (minor[piece] - d) % RING).wait_recv()
        for i in range(SUBS):
            for way in range(2):
                hop(piece, way, 1, turned(way, i), False).start()
    for piece in range(2):
        share_own(piece, c).start()

    plan_steps(tok, total, w * TOK, PLAN_A, TOK * 64 // PLAN)

    moves = []
    for k in range(1, 5):
        for i in range(SUBS):
            for piece in range(2):
                for way in range(2):
                    if k < 4 or i < SUBS // 2:
                        moves.append((piece, way, k, turned(way, i), k < 3 or (k == 3 and i < SUBS // 2)))
    for piece, way, k, h, onward in moves:
        hop(piece, way, k, h, True).wait_recv()
        if onward:
            hop(piece, way, k + 1, h, False).start()
        share(piece, way, k, h, c).start()

    plan_words(total, clip_starts(clip_s), words, entry)

    to_sibling().wait_send()

    @pl.when(near_ok)
    def _():
        to_near(0).wait_send()
        to_near(1).wait_send()

    for piece in range(2):
        for d in order:
            first_hop(piece, d, minor[piece]).wait_send()
        share_own(piece, c).wait_send()
        share_own(piece, 1 - c).wait_recv()
    for piece, way, k, h, onward in moves:
        hop(piece, way, k, h, False).wait_send()
        share(piece, way, k, h, c).wait_send()
        share(piece, way, k, h, 1 - c).wait_recv()


PLAN_A = 40


def gather_tables(pixel_slabs, clip_lengths, tok_place):
    perm, pick = placement_tables()
    dma = pltpu.SemaphoreType.DMA
    vmem = pl.BlockSpec(memory_space=pltpu.VMEM)
    shape = (2, 2, RING, RING, 64, 128)
    return pl.pallas_call(
        gather_kernel,
        out_shape=(
            jax.ShapeDtypeStruct(shape, BF),
            jax.ShapeDtypeStruct((24, 128), jnp.int32),
            jax.ShapeDtypeStruct((8, 128), jnp.int32),
        ),
        in_specs=[pl.BlockSpec(memory_space=pltpu.SMEM), vmem, vmem, vmem, vmem],
        out_specs=(pl.BlockSpec(memory_space=pl.ANY), vmem, vmem),
        scratch_shapes=[
            pltpu.VMEM((2, 64, 128), BF),
            pltpu.VMEM((3, 2, 3, 8, 128), BF),
            pltpu.VMEM((64, 32), F32),
            dma((3,)),
            dma((3,)),
            dma((2, RING)),
            dma((2, RING)),
            dma((2,)),
            dma((2, 2, 4, SUBS)),
            dma((2, 2, 4, SUBS)),
            dma((2, 2, 4, SUBS)),
            dma((2, 2, 4, SUBS)),
            dma((2,)),
            dma((2,)),
        ],
        compiler_params=pltpu.CompilerParams(
            collective_id=0, has_side_effects=True, vmem_limit_bytes=12 << 20
        ),
        name="gather_tables",
    )(
        clip_lengths,
        pixel_slabs,
        tok_place.reshape(512, 128),
        jnp.asarray(perm, BF),
        jnp.asarray(pick, BF),
    )


TILE = 1024
BATCH = 32


def column(row):
    n = row.shape[1]
    same = lax.broadcasted_iota(jnp.int32, (n, n), 0) == lax.broadcasted_iota(jnp.int32, (n, n), 1)
    return jnp.sum(jnp.where(same, jnp.broadcast_to(row, (n, n)), 0.0), axis=1, keepdims=True)


def main_kernel(
    words,
    slab_s,
    clip_s,
    entry,
    table,
    spread_all,
    in_weight,
    in_bias,
    gain,
    weight,
    bias,
    out,
    spread,
    frames,
    patches,
    shifts,
    w1,
    w2,
    hid,
    act,
    spread_sem,
):
    n = lax.axis_index("narrow")
    c = n % 2

    fetch = pltpu.make_async_copy(spread_all.at[c], spread, spread_sem)
    fetch.start()

    zero = jnp.zeros((CH, CH), F32)
    for kt in range(3):
        for dy in range(2):
            for dx in range(2):
                blocks = []
                for ry in range(4):
                    for rx in range(4):
                        ky, kx = ry - dy, rx - dx
                        within = 0 <= ky < 3 and 0 <= kx < 3
                        blocks.append(
                            weight[ky, kx, :, kt * CH : (kt + 1) * CH].astype(F32) if within else zero
                        )
                row = (dy * 2 + dx) * CH
                w2[kt, row : row + CH, :] = jnp.concatenate(blocks, axis=1).astype(BF)

    half_gain = column(gain[...]) * 0.5
    out_bias = column(bias[...])
    rest = in_bias[...]
    split = []
    for _ in range(3):
        part = rest.astype(BF).astype(F32)
        split.append(part)
        rest = rest - part
    taps = [in_weight[ky, i].astype(F32) for ky in range(3) for i in range(9)]
    taps = jnp.transpose(jnp.concatenate(taps + split, axis=0)).astype(BF)
    lane = lax.broadcasted_iota(jnp.int32, (8, 128), 1)
    for j in range(4):
        shifts[8 * j : 8 * j + 8, :] = (lane + 256 - (48 * c + 12 * j)) & 127
    fetch.wait()
    for pos in range(16):
        w1[pos * CH : (pos + 1) * CH, :] = lax.dot_general(
            taps, spread[:, pos * 384 : (pos + 1) * 384], NN, preferred_element_type=F32
        ).astype(BF)

    frames[0 : LEAD * FRAME_ROWS, :] = jnp.zeros((LEAD * FRAME_ROWS, 128), F32)
    frames[(LEAD + 256) * FRAME_ROWS : (LEAD + 256) * FRAME_ROWS + 8, :] = jnp.zeros((8, 128), F32)
    for k in range(8):
        piece, core = k // 4, (k // 2) % 2

        def fill(m, carry):
            maj = (k % 2) * 4 + m
            at = []
            for mnr in range(RING):
                wide = maj * RING + mnr if piece == 0 else mnr * RING + maj
                frame = slab_s[wide * 4 + core * 2 + piece]
                at.append(pl.multiple_of((frame + LEAD) * FRAME_ROWS, 8))
            for mnr in range(RING):
                frames[pl.ds(at[mnr], 8), :] = jnp.zeros((8, 128), F32)
                frames[pl.ds(at[mnr] + 8, 64), :] = table[32 * k + m * RING + mnr].astype(F32)
            return carry

        lax.fori_loop(0, 4, fill, 0)

    late = lax.broadcasted_iota(jnp.int32, (5, 128), 0)

    def pick_up(s):
        base, j, least = words[s], words[TOK + s], words[2 * TOK + s]
        rel = shifts[pl.ds(pl.multiple_of(j * 8, 8), 5), :]
        left = frames[pl.ds(base, 5, stride=FRAME_ROWS), :]
        mid = pltpu.roll(frames[pl.ds(base + 1, 5, stride=FRAME_ROWS), :], 36, 1)
        right = pltpu.roll(frames[pl.ds(base + 2, 5, stride=FRAME_ROWS), :], 72, 1)
        row = jnp.where(rel < 36, left, jnp.where(rel < 72, mid, jnp.where(rel < 108, right, 1.0)))
        row = jnp.where(late >= least, row, 0.0)
        return pltpu.roll(row, 128 - 12 * j, 1)

    def pull(q, carry):
        rows = [pick_up(q * BATCH + i) for i in range(BATCH)]
        for i in range(BATCH):
            patches[pl.ds(q * BATCH + i, 5, stride=TOK), :] = rows[i]
        return carry

    lax.fori_loop(0, TOK // BATCH, pull, 0)

    starts = clip_starts(clip_s)

    def tile(g, carry):
        at = pl.multiple_of(g * TILE, TILE)
        e = jnp.concatenate([entry[pl.ds(g * (TILE // 128) + i, 1), :] for i in range(TILE // 128)], axis=1)
        t, j, col = e >> 8, (e >> 6) & 3, e & 63
        age = clip_age(starts, t)
        row_ok = [
            jnp.logical_not(jnp.logical_and(j == 0, n == 0)),
            None,
            None,
            jnp.logical_not(jnp.logical_and(j == 3, n == 7)),
        ]
        col_ok = [col != 0, None, None, col != 63]
        total = jnp.concatenate([jnp.broadcast_to(out_bias, (CH, TILE))] * 4, axis=0)
        for s in range(3):
            block = jnp.concatenate(
                [patches[pl.ds(pl.multiple_of((s + kt) * TOK + at, TILE), TILE), :].astype(BF) for kt in range(3)],
                axis=1,
            )
            hid[...] = lax.dot_general(w1[...], block, NT, preferred_element_type=F32)
            for ry in range(4):
                for rx in range(4):
                    pos = ry * 4 + rx
                    h = hid[pos * CH : (pos + 1) * CH, :]
                    scale = lax.rsqrt(jnp.sum(h * h, axis=0, keepdims=True) * (1.0 / CH) + EPSILON)
                    ok = age >= 2 - s
                    if row_ok[ry] is not None:
                        ok = jnp.logical_and(ok, row_ok[ry])
                    if col_ok[rx] is not None:
                        ok = jnp.logical_and(ok, col_ok[rx])
                    u = h * jnp.where(ok, scale, 0.0) * half_gain
                    act[pos * CH : (pos + 1) * CH, :] = (u + u * jnp.tanh(u)).astype(BF)
            total = total + lax.dot_general(w2[s], act[...], NN, preferred_element_type=F32)
            if s == 2:
                keep = [hid[(ry * 4 + rx) * CH : (ry * 4 + rx + 1) * CH, :] for ry in (1, 2) for rx in (1, 2)]
                total = total + jnp.concatenate(keep, axis=0)
        out[pl.ds(at, TILE), :] = jnp.transpose(total).astype(BF)
        return carry

    lax.fori_loop(0, TOK // TILE, tile, 0)


def encode(words, entry, slab_place, clip_lengths, table, in_weight, in_bias, gain, weight, bias):
    vmem = pl.BlockSpec(memory_space=pltpu.VMEM)
    smem = pl.BlockSpec(memory_space=pltpu.SMEM)
    anywhere = pl.BlockSpec(memory_space=pl.ANY)
    return pl.pallas_call(
        main_kernel,
        out_shape=jax.ShapeDtypeStruct((TOK, 4 * CH), BF),
        in_specs=[smem, smem, smem, vmem, vmem, anywhere] + [vmem] * 5,
        out_specs=vmem,
        scratch_shapes=[
            pltpu.VMEM((84, 16 * 384), BF),
            pltpu.VMEM(((LEAD + 256) * FRAME_ROWS + 8, 128), F32),
            pltpu.VMEM((5 * TOK, 128), F32),
            pltpu.VMEM((32, 128), jnp.int32),
            pltpu.VMEM((16 * CH, 384), BF),
            pltpu.VMEM((3, 4 * CH, 16 * CH), BF),
            pltpu.VMEM((16 * CH, TILE), F32),
            pltpu.VMEM((16 * CH, TILE), BF),
            pltpu.SemaphoreType.DMA,
        ],
        compiler_params=pltpu.CompilerParams(vmem_limit_bytes=44 << 20),
        name="encode",
    )(
        words.reshape(3 * TOK),
        slab_place,
        clip_lengths,
        entry,
        table,
        jnp.asarray(weight_table(), BF),
        in_weight,
        in_bias.reshape(1, CH),
        gain.reshape(1, CH),
        weight,
        bias.reshape(1, CH),
    )


def body(
    pixel_slabs,
    conv_in_weight,
    conv_in_bias,
    norm_gain,
    conv_weight,
    conv_bias,
    clip_lengths,
    slab_place,
    tok_place,
):
    table, words, entry = gather_tables(pixel_slabs, clip_lengths, tok_place)
    return encode(
        words,
        entry,
        slab_place,
        clip_lengths,
        table.reshape(256, 64, 128),
        jnp.transpose(conv_in_weight, (0, 3, 1, 2)),
        conv_in_bias,
        norm_gain,
        conv_weight,
        conv_bias,
    )


def solution(mesh):
    placed = (P("wide", None, "narrow", None), P(), P(), P(), P(), P(), P(), P(), P())
    return jax.shard_map(
        body, mesh=mesh, in_specs=placed, out_specs=P(("wide", "narrow"), None), check_vma=False
    )
```

```python
import jax
import jax.numpy as jnp
import numpy as np
from jax import lax
from jax.experimental import pallas as pl
from jax.experimental.pallas import tpu as pltpu
from jax.sharding import PartitionSpec as P

EPSILON = 1e-06
MESH = pl.DeviceIdType.MESH
BF = jnp.bfloat16
F32 = jnp.float32
RING = 8
CH = 96
TOK = 1024
FRAME_ROWS = 72
LEAD = 4
NT = (((1,), (1,)), ((), ()))
NN = (((1,), (0,)), ((), ()))


def placement_tables():
    perm = np.zeros((256, 96), np.float32)
    for row in range(20):
        region, inner = (0, 6 + row) if row < 2 else ((1, row - 2) if row < 10 else ((2, row - 10) if row < 18 else (3, row - 18)))
        for parity in range(2):
            for ch in range(3):
                perm[parity * 128 + row * 6 + parity * 3 + ch, region * 24 + ch * 8 + inner] = 1
    pick = np.zeros((2, 64, 128), np.float32)
    for parity in range(2):
        for pair in range(64):
            pick[parity, pair, 2 * pair + parity] = 1
    return perm, pick


def weight_table():
    table = np.zeros((2, 84, 16 * 384), np.float32)
    for core in range(2):
        for ry in range(4):
            for rx in range(4):
                base = (ry * 4 + rx) * 384
                for ky in range(3):
                    for kx in range(3):
                        for kt in range(3):
                            for ch in range(3):
                                row, col = ry + ky, rx + kx
                                lane = (col // 2) * 36 + row * 6 + (col % 2) * 3 + ch
                                lane = (lane + 48 * core) % 128
                                table[core, (ky * 9 + kt * 3 + ch) * 3 + kx, base + kt * 128 + lane] = 1
                for part in range(3):
                    table[core, 81 + part, base + 2 * 128 + (108 + part + 48 * core) % 128] = 1
    return table


def clip_age(starts, t):
    latest = jnp.zeros_like(t)
    for i in range(1, 6):
        latest = jnp.where(starts[i] <= t, starts[i], latest)
    return t - latest


def clip_starts(clip_s):
    starts = [jnp.int32(0)]
    for i in range(5):
        starts.append(starts[-1] + clip_s[i])
    return starts


PLAN = 1024


def plan_steps(tok, total, base, first, last):
    sub = lax.broadcasted_iota(jnp.int32, (32, PLAN), 0)
    high_of = (sub % 8) * 4 + sub // 8
    lane = lax.broadcasted_iota(jnp.int32, (32, PLAN), 1)
    inside = (lane % 256).astype(F32)
    frame = (lane // 256).astype(F32)

    def step(q, carry):
        rows = tok[pl.ds(pl.multiple_of(q * 8, 8), 8), :] - base
        row = jnp.concatenate([jnp.broadcast_to(rows[i : i + 1], (32, 128)) for i in range(8)], axis=1)
        hit = row >> 5 == high_of
        times = jnp.where(hit, frame + (q * (PLAN // 256)).astype(F32), 0.0)
        inner = jnp.where(hit, inside, 0.0)
        left = jnp.concatenate([times, inner], axis=0).astype(BF)
        right = jnp.where(row & 31 == sub, 1.0, 0.0).astype(BF)
        total[...] += lax.dot_general(left, right, NT, preferred_element_type=F32)
        return carry

    lax.fori_loop(first, last, step, 0)


def plan_words(total, starts, words, entry):
    found = (total[:32, :] * 256.0 + total[32:, :]).astype(jnp.int32)
    e = jnp.concatenate([found[8 * m : 8 * m + 8] for m in range(4)], axis=1)
    entry[...] = e
    t, j, col = e >> 8, (e >> 6) & 3, e & 63
    words[0:8, :] = t * FRAME_ROWS + 7 + col
    words[8:16, :] = j
    words[16:24, :] = 4 - clip_age(starts, t)


def lay_weights(in_weight, in_bias, weight, spread, w1, w2):
    zero = jnp.zeros((CH, CH), F32)
    for kt in range(3):
        for dy in range(2):
            for dx in range(2):
                blocks = []
                for ry in range(4):
                    for rx in range(4):
                        ky, kx = ry - dy, rx - dx
                        within = 0 <= ky < 3 and 0 <= kx < 3
                        blocks.append(
                            weight[ky, kx, :, kt * CH : (kt + 1) * CH].astype(F32) if within else zero
                        )
                row = (dy * 2 + dx) * CH
                w2[kt, row : row + CH, :] = jnp.concatenate(blocks, axis=1).astype(BF)
    rest = in_bias[...]
    split = []
    for _ in range(3):
        part = rest.astype(BF).astype(F32)
        split.append(part)
        rest = rest - part
    taps = [in_weight[ky, i].astype(F32) for ky in range(3) for i in range(9)]
    taps = jnp.transpose(jnp.concatenate(taps + split, axis=0)).astype(BF)
    for pos in range(16):
        w1[pos * CH : (pos + 1) * CH, :] = lax.dot_general(
            taps, spread[:, pos * 384 : (pos + 1) * 384], NN, preferred_element_type=F32
        ).astype(BF)


SUBS = 2


def gather_kernel(
    clip_hbm,
    slab_hbm,
    pix,
    tok_hbm,
    perm_hbm,
    pick_hbm,
    spread_hbm,
    in_weight_hbm,
    in_bias_hbm,
    gain_hbm,
    weight_hbm,
    bias_hbm,
    out,
    words,
    entry,
    scales,
    w1,
    w2,
    clip_s,
    slab,
    mine_v,
    tok,
    perm,
    pick,
    spread,
    in_weight,
    in_bias,
    gain,
    weight,
    bias,
    load_sem,
    own,
    edge,
    total,
    s0,
    r0,
    s1,
    r1,
    keep,
    s2,
    r2,
    s3,
    r3,
    s4,
    r4,
):
    w = lax.axis_index("wide")
    n = lax.axis_index("narrow")
    z, y = w // RING, w % RING
    x, c = n // 2, n % 2
    sibling = (w, x * 2 + 1 - c)
    near = x + 2 * c - 1
    near_ok = jnp.logical_and(near >= 0, near <= 3)
    major = (z, y)
    minor = (y, z)

    def wide_of(piece, maj, mnr):
        return maj * RING + mnr if piece == 0 else mnr * RING + maj

    def along_minor(piece, d):
        return (wide_of(piece, major[piece], (minor[piece] + d) % RING), n)

    def along_major(piece, d):
        return (wide_of(piece, (major[piece] + d) % RING, minor[piece]), n)

    pairs = [
        (pix.at[pl.ds(2 * c, 2)], mine_v),
        (perm_hbm, perm),
        (pick_hbm, pick),
        (tok_hbm, tok),
        (spread_hbm.at[c], spread),
        (in_weight_hbm, in_weight),
        (in_bias_hbm, in_bias),
        (weight_hbm, weight),
        (clip_hbm, clip_s),
        (slab_hbm, slab),
        (gain_hbm, gain),
        (bias_hbm, bias),
    ]
    loads = [pltpu.make_async_copy(src, dst, load_sem.at[i]) for i, (src, dst) in enumerate(pairs)]
    for copy in loads:
        copy.start()

    barrier = pltpu.get_barrier_semaphore()
    pl.semaphore_signal(barrier, inc=1, device_id=sibling, device_id_type=MESH)
    for piece in range(2):
        for d in range(1, RING):
            pl.semaphore_signal(barrier, inc=1, device_id=along_minor(piece, d), device_id_type=MESH)

    for side in (1, 3):
        for core in range(2):
            beside = ((x + side) % 4) * 2 + core
            pl.semaphore_signal(barrier, inc=1, device_id=(w, beside), device_id_type=MESH)
    pl.semaphore_wait(barrier, 19)

    def to_sibling():
        return pltpu.make_async_remote_copy(
            pix.at[pl.ds(2 * (1 - c), 2)], edge.at[0], s0.at[0], r0.at[0], sibling, MESH
        )

    def to_near(core):
        return pltpu.make_async_remote_copy(
            pix.at[pl.ds(2 * core, 2)],
            edge.at[2 - c],
            s0.at[1 + core],
            r0.at[2 - c],
            (w, jnp.clip(near, 0, 3) * 2 + core),
            MESH,
        )

    def arrival(region):
        return pltpu.make_async_remote_copy(
            pix.at[pl.ds(0, 2)], edge.at[region], s0.at[0], r0.at[region], sibling, MESH
        )

    to_sibling().start()

    @pl.when(near_ok)
    def _():
        to_near(0).start()
        to_near(1).start()

    @pl.when(x == 0)
    def _():
        edge[1] = jnp.zeros_like(edge[1])

    @pl.when(x == 3)
    def _():
        edge[2] = jnp.zeros_like(edge[2])

    arrival(0).wait_recv()

    @pl.when(x > 0)
    def _():
        arrival(1).wait_recv()

    @pl.when(x < 3)
    def _():
        arrival(2).wait_recv()

    for copy in loads[:3]:
        copy.wait()
    for piece in range(2):
        mine = mine_v[piece].astype(F32).reshape(24, 128)
        other = edge[0, piece].astype(F32).reshape(24, 128)
        low = edge[1, piece].astype(F32).reshape(24, 128)
        high = edge[2, piece].astype(F32).reshape(24, 128)
        first = jnp.where(c == 0, mine, other)
        second = jnp.where(c == 0, other, mine)
        stack = jnp.concatenate([low, first, second, high], axis=0).astype(BF)
        laid = lax.dot_general(perm[...], stack, NN, preferred_element_type=F32).astype(BF)
        rows = lax.dot_general(pick[0], laid[:128], NT, preferred_element_type=F32)
        rows += lax.dot_general(pick[1], laid[128:], NT, preferred_element_type=F32)
        own[piece] = rows.astype(BF)

    def local(piece):
        return pltpu.make_async_copy(own.at[piece], out.at[piece, c, major[piece], minor[piece]], keep.at[piece])

    def first_hop(piece, d, slot):
        return pltpu.make_async_remote_copy(
            own.at[piece],
            out.at[piece, c, major[piece], slot],
            s1.at[piece, d],
            r1.at[piece, d],
            along_minor(piece, d),
            MESH,
        )

    order = (4, 3, 5, 2, 6, 1, 7)
    for piece in range(2):
        for d in order:
            first_hop(piece, d, minor[piece]).start()
    for piece in range(2):
        local(piece).start()

    for copy in loads[3:]:
        copy.wait()
    total[...] = jnp.zeros_like(total)
    plan_steps(tok, total, w * TOK, 0, TOK * 64 // PLAN)
    plan_words(total, clip_starts(clip_s), words, entry)
    words[24:26, :] = slab[...]
    scales[0:1, 0:CH] = gain[...]
    scales[1:2, 0:CH] = bias[...]
    lay_weights(in_weight, in_bias, weight, spread, w1, w2)

    part = RING // SUBS

    def hop(piece, way, k, h, arrived):
        step = 1 - 2 * way
        chunk = (major[piece] - step * (k if arrived else k - 1)) % RING
        ref = out.at[piece, c, chunk, pl.ds(part * h, part)]
        return pltpu.make_async_remote_copy(
            ref, ref, s2.at[piece, way, k - 1, h], r2.at[piece, way, k - 1, h], along_major(piece, step), MESH
        )

    def share(piece, way, k, h, core):
        chunk = (major[piece] - (1 - 2 * way) * k) % RING
        where = (piece, core, chunk, pl.ds(part * h, part))
        return pltpu.make_async_remote_copy(
            out.at[where], out.at[where], s3.at[piece, way, k - 1, h], r3.at[piece, way, k - 1, h], sibling, MESH
        )

    def share_own(piece, core):
        where = (piece, core, major[piece])
        return pltpu.make_async_remote_copy(out.at[where], out.at[where], s4.at[piece], r4.at[piece], sibling, MESH)

    def turned(way, i):
        return i if way == 0 else SUBS - 1 - i

    for piece in range(2):
        local(piece).wait()
        for d in reversed(order):
            first_hop(piece, d, (minor[piece] - d) % RING).wait_recv()
        for i in range(SUBS):
            for way in range(2):
                hop(piece, way, 1, turned(way, i), False).start()
    for piece in range(2):
        share_own(piece, c).start()

    moves = []
    for k in range(1, 5):
        for i in range(SUBS):
            for piece in range(2):
                for way in range(2):
                    if k < 4 or i < SUBS // 2:
                        moves.append((piece, way, k, turned(way, i), k < 3 or (k == 3 and i < SUBS // 2)))
    for piece, way, k, h, onward in moves:
        hop(piece, way, k, h, True).wait_recv()
        if onward:
            hop(piece, way, k + 1, h, False).start()
        share(piece, way, k, h, c).start()

    to_sibling().wait_send()

    @pl.when(near_ok)
    def _():
        to_near(0).wait_send()
        to_near(1).wait_send()

    for piece in range(2):
        for d in order:
            first_hop(piece, d, minor[piece]).wait_send()
        share_own(piece, c).wait_send()
        share_own(piece, 1 - c).wait_recv()
    for piece, way, k, h, onward in moves:
        hop(piece, way, k, h, False).wait_send()
        share(piece, way, k, h, c).wait_send()
        share(piece, way, k, h, 1 - c).wait_recv()


def gather_tables(clip_lengths, slab_place, pixel_slabs, tok_place, in_weight, in_bias, gain, weight, bias):
    perm, pick = placement_tables()
    dma = pltpu.SemaphoreType.DMA
    vmem = pl.BlockSpec(memory_space=pltpu.VMEM)
    shape = (2, 2, RING, RING, 64, 128)
    return pl.pallas_call(
        gather_kernel,
        out_shape=(
            jax.ShapeDtypeStruct(shape, BF),
            jax.ShapeDtypeStruct((32, 128), jnp.int32),
            jax.ShapeDtypeStruct((8, 128), jnp.int32),
            jax.ShapeDtypeStruct((8, 128), F32),
            jax.ShapeDtypeStruct((16 * CH, 384), BF),
            jax.ShapeDtypeStruct((3, 4 * CH, 16 * CH), BF),
        ),
        in_specs=[pl.BlockSpec(memory_space=pltpu.HBM)] * 12,
        out_specs=(pl.BlockSpec(memory_space=pl.ANY), vmem, vmem, vmem, vmem, vmem),
        scratch_shapes=[
            pltpu.SMEM((6,), jnp.int32),
            pltpu.VMEM((2, 128), jnp.int32),
            pltpu.VMEM((2, 3, 8, 128), BF),
            pltpu.VMEM((512, 128), jnp.int32),
            pltpu.VMEM((256, 96), BF),
            pltpu.VMEM((2, 64, 128), BF),
            pltpu.VMEM((84, 16 * 384), BF),
            pltpu.VMEM((3, 9, 3, CH), BF),
            pltpu.VMEM((1, CH), F32),
            pltpu.VMEM((1, CH), F32),
            pltpu.VMEM((3, 3, CH, 3 * CH), BF),
            pltpu.VMEM((1, CH), F32),
            dma((12,)),
            pltpu.VMEM((2, 64, 128), BF),
            pltpu.VMEM((3, 2, 3, 8, 128), BF),
            pltpu.VMEM((64, 32), F32),
            dma((3,)),
            dma((3,)),
            dma((2, RING)),
            dma((2, RING)),
            dma((2,)),
            dma((2, 2, 4, SUBS)),
            dma((2, 2, 4, SUBS)),
            dma((2, 2, 4, SUBS)),
            dma((2, 2, 4, SUBS)),
            dma((2,)),
            dma((2,)),
        ],
        compiler_params=pltpu.CompilerParams(
            collective_id=0, has_side_effects=True, vmem_limit_bytes=16 << 20
        ),
        name="gather_tables",
    )(
        *[pltpu.with_memory_space_constraint(v, pltpu.HBM) for v in (
        clip_lengths,
        slab_place.reshape(2, 128),
        pixel_slabs,
        tok_place.reshape(512, 128),
        jnp.asarray(perm, BF),
        jnp.asarray(pick, BF),
        jnp.asarray(weight_table(), BF),
        jnp.transpose(in_weight, (0, 3, 1, 2)),
        in_bias.reshape(1, CH),
        gain.reshape(1, CH),
        weight,
        bias.reshape(1, CH),
        )]
    )


TILE = 1024
BATCH = 32


def column(row):
    n = row.shape[1]
    same = lax.broadcasted_iota(jnp.int32, (n, n), 0) == lax.broadcasted_iota(jnp.int32, (n, n), 1)
    return jnp.sum(jnp.where(same, jnp.broadcast_to(row, (n, n)), 0.0), axis=1, keepdims=True)


def main_kernel(words, entry, least, table, scales, w1, w2, out, frames, patches, shifts, hid, act):
    n = lax.axis_index("narrow")
    c = n % 2

    half_gain = column(scales[0:1, 0:CH]) * 0.5
    out_bias = column(scales[1:2, 0:CH])
    lane = lax.broadcasted_iota(jnp.int32, (8, 128), 1)
    for j in range(4):
        shifts[8 * j : 8 * j + 8, :] = (lane + 256 - (48 * c + 12 * j)) & 127

    frames[0 : LEAD * FRAME_ROWS, :] = jnp.zeros((LEAD * FRAME_ROWS, 128), F32)
    frames[(LEAD + 256) * FRAME_ROWS : (LEAD + 256) * FRAME_ROWS + 8, :] = jnp.zeros((8, 128), F32)
    for k in range(8):
        piece, core = k // 4, (k // 2) % 2

        def fill(m, carry):
            maj = (k % 2) * 4 + m
            at = []
            for mnr in range(RING):
                wide = maj * RING + mnr if piece == 0 else mnr * RING + maj
                frame = words[3 * TOK + wide * 4 + core * 2 + piece]
                at.append(pl.multiple_of((frame + LEAD) * FRAME_ROWS, 8))
            for mnr in range(RING):
                frames[pl.ds(at[mnr], 8), :] = jnp.zeros((8, 128), F32)
                frames[pl.ds(at[mnr] + 8, 64), :] = table[32 * k + m * RING + mnr].astype(F32)
            return carry

        lax.fori_loop(0, 4, fill, 0)

    late = lax.broadcasted_iota(jnp.int32, (5, 128), 0)

    def pick_up(s):
        base, j, oldest = words[s], words[TOK + s], words[2 * TOK + s]
        rel = shifts[pl.ds(pl.multiple_of(j * 8, 8), 5), :]
        left = frames[pl.ds(base, 5, stride=FRAME_ROWS), :]
        mid = pltpu.roll(frames[pl.ds(base + 1, 5, stride=FRAME_ROWS), :], 36, 1)
        right = pltpu.roll(frames[pl.ds(base + 2, 5, stride=FRAME_ROWS), :], 72, 1)
        row = jnp.where(rel < 36, left, jnp.where(rel < 72, mid, jnp.where(rel < 108, right, 1.0)))
        row = jnp.where(late >= oldest, row, 0.0)
        return pltpu.roll(row, 128 - 12 * j, 1)

    def pull(q, carry):
        rows = [pick_up(q * BATCH + i) for i in range(BATCH)]
        for i in range(BATCH):
            patches[pl.ds(q * BATCH + i, 5, stride=TOK), :] = rows[i]
        return carry

    lax.fori_loop(0, TOK // BATCH, pull, 0)

    def tile(g, carry):
        at = pl.multiple_of(g * TILE, TILE)
        e, old = [
            jnp.concatenate([ref[pl.ds(g * (TILE // 128) + i, 1), :] for i in range(TILE // 128)], axis=1)
            for ref in (entry, least.at[pl.ds(16, 8)])
        ]
        j, col, age = (e >> 6) & 3, e & 63, 4 - old
        row_ok = [
            jnp.logical_not(jnp.logical_and(j == 0, n == 0)),
            None,
            None,
            jnp.logical_not(jnp.logical_and(j == 3, n == 7)),
        ]
        col_ok = [col != 0, None, None, col != 63]
        total = jnp.concatenate([jnp.broadcast_to(out_bias, (CH, TILE))] * 4, axis=0)
        for s in range(3):
            block = jnp.concatenate(
                [patches[pl.ds(pl.multiple_of((s + kt) * TOK + at, TILE), TILE), :].astype(BF) for kt in range(3)],
                axis=1,
            )
            hid[...] = lax.dot_general(w1[...], block, NT, preferred_element_type=F32)
            for ry in range(4):
                for rx in range(4):
                    pos = ry * 4 + rx
                    h = hid[pos * CH : (pos + 1) * CH, :]
                    scale = lax.rsqrt(jnp.sum(h * h, axis=0, keepdims=True) * (1.0 / CH) + EPSILON)
                    ok = age >= 2 - s
                    if row_ok[ry] is not None:
                        ok = jnp.logical_and(ok, row_ok[ry])
                    if col_ok[rx] is not None:
                        ok = jnp.logical_and(ok, col_ok[rx])
                    u = h * jnp.where(ok, scale, 0.0) * half_gain
                    act[pos * CH : (pos + 1) * CH, :] = (u + u * jnp.tanh(u)).astype(BF)
            total = total + lax.dot_general(w2[s], act[...], NN, preferred_element_type=F32)
            if s == 2:
                keep = [hid[(ry * 4 + rx) * CH : (ry * 4 + rx + 1) * CH, :] for ry in (1, 2) for rx in (1, 2)]
                total = total + jnp.concatenate(keep, axis=0)
        out[pl.ds(at, TILE), :] = jnp.transpose(total).astype(BF)
        return carry

    lax.fori_loop(0, TOK // TILE, tile, 0)


def encode(words, entry, table, scales, w1, w2):
    vmem = pl.BlockSpec(memory_space=pltpu.VMEM)
    return pl.pallas_call(
        main_kernel,
        out_shape=jax.ShapeDtypeStruct((TOK, 4 * CH), BF),
        in_specs=[pl.BlockSpec(memory_space=pltpu.SMEM)] + [vmem] * 6,
        out_specs=vmem,
        scratch_shapes=[
            pltpu.VMEM(((LEAD + 256) * FRAME_ROWS + 8, 128), F32),
            pltpu.VMEM((5 * TOK, 128), F32),
            pltpu.VMEM((32, 128), jnp.int32),
            pltpu.VMEM((16 * CH, TILE), F32),
            pltpu.VMEM((16 * CH, TILE), BF),
        ],
        compiler_params=pltpu.CompilerParams(vmem_limit_bytes=42 << 20),
        name="encode",
    )(words.reshape(4 * TOK), entry, words, table.reshape(256, 64, 128), scales, w1, w2)


def body(
    pixel_slabs,
    conv_in_weight,
    conv_in_bias,
    norm_gain,
    conv_weight,
    conv_bias,
    clip_lengths,
    slab_place,
    tok_place,
):
    table, words, entry, scales, w1, w2 = gather_tables(
        clip_lengths,
        slab_place,
        pixel_slabs,
        tok_place,
        conv_in_weight,
        conv_in_bias,
        norm_gain,
        conv_weight,
        conv_bias,
    )
    return encode(words, entry, table, scales, w1, w2)


def solution(mesh):
    placed = (P("wide", None, "narrow", None), P(), P(), P(), P(), P(), P(), P(), P())
    return jax.shard_map(
        body, mesh=mesh, in_specs=placed, out_specs=P(("wide", "narrow"), None), check_vma=False
    )
```

```python
import functools

import jax
import jax.numpy as jnp
import numpy as np
from jax import lax
from jax.experimental import pallas as pl
from jax.experimental.pallas import tpu as pltpu
from jax.sharding import PartitionSpec as P

EPSILON = 1e-06
MESH = pl.DeviceIdType.MESH
BF = jnp.bfloat16
F32 = jnp.float32
RING = 8
CH = 96
TOK = 1024
FRAME_ROWS = 72
LEAD = 4
NT = (((1,), (1,)), ((), ()))
NN = (((1,), (0,)), ((), ()))


def placement_tables():
    perm = np.zeros((256, 96), np.float32)
    for row in range(20):
        region, inner = (0, 6 + row) if row < 2 else ((1, row - 2) if row < 10 else ((2, row - 10) if row < 18 else (3, row - 18)))
        for parity in range(2):
            for ch in range(3):
                perm[parity * 128 + row * 6 + parity * 3 + ch, region * 24 + ch * 8 + inner] = 1
    pick = np.zeros((2, 64, 128), np.float32)
    for parity in range(2):
        for pair in range(64):
            pick[parity, pair, 2 * pair + parity] = 1
    return perm, pick


def weight_table():
    table = np.zeros((2, 84, 16 * 384), np.float32)
    for core in range(2):
        for ry in range(4):
            for rx in range(4):
                base = (ry * 4 + rx) * 384
                for ky in range(3):
                    for kx in range(3):
                        for kt in range(3):
                            for ch in range(3):
                                row, col = ry + ky, rx + kx
                                lane = (col // 2) * 36 + row * 6 + (col % 2) * 3 + ch
                                lane = (lane + 48 * core) % 128
                                table[core, (ky * 9 + kt * 3 + ch) * 3 + kx, base + kt * 128 + lane] = 1
                for part in range(3):
                    table[core, 81 + part, base + 2 * 128 + (108 + part + 48 * core) % 128] = 1
    return table


def clip_age(starts, t):
    latest = jnp.zeros_like(t)
    for i in range(1, 6):
        latest = jnp.where(starts[i] <= t, starts[i], latest)
    return t - latest


def clip_starts(clip_s):
    starts = [jnp.int32(0)]
    for i in range(5):
        starts.append(starts[-1] + clip_s[i])
    return starts


PLAN = 1024


def plan_steps(tok, total, base, first, last):
    sub = lax.broadcasted_iota(jnp.int32, (32, PLAN), 0)
    high_of = ((sub % 8) * 4 + sub // 8).astype(F32).astype(BF)
    low_of = sub.astype(F32).astype(BF)
    lane = lax.broadcasted_iota(jnp.int32, (32, PLAN), 1)
    inside = (lane % 256).astype(F32).astype(BF)
    frame = (lane // 256).astype(F32)
    none = jnp.zeros((32, PLAN), BF)
    ones = jnp.ones((32, PLAN), BF)

    def spread_rows(rows):
        wide = [jnp.broadcast_to(rows[i : i + 1], (32, 128)).astype(BF) for i in range(8)]
        return jnp.concatenate(wide, axis=1)

    def step(q, carry):
        rows = tok[pl.ds(pl.multiple_of(q * 8, 8), 8), :] - base
        high = spread_rows(jnp.clip(rows >> 5, -1, 64).astype(F32))
        low = spread_rows((rows & 31).astype(F32))
        hit = high == high_of
        times = jnp.where(hit, (frame + (q * (PLAN // 256)).astype(F32)).astype(BF), none)
        left = jnp.concatenate([times, jnp.where(hit, inside, none)], axis=0)
        right = jnp.where(low == low_of, ones, none)
        total[...] += lax.dot_general(left, right, NT, preferred_element_type=F32)
        return carry

    lax.fori_loop(first, last, step, 0, unroll=4)


def plan_words(total, starts, words, entry):
    found = (total[:32, :] * 256.0 + total[32:, :]).astype(jnp.int32)
    e = jnp.concatenate([found[8 * m : 8 * m + 8] for m in range(4)], axis=1)
    entry[...] = e
    t, j, col = e >> 8, (e >> 6) & 3, e & 63
    words[0:8, :] = t * FRAME_ROWS + 7 + col
    words[8:16, :] = j
    words[16:24, :] = 4 - clip_age(starts, t)


def lay_second(weight, w2, kt, dy, dx):
    zero = jnp.zeros((CH, CH), F32)
    blocks = []
    for ry in range(4):
        for rx in range(4):
            ky, kx = ry - dy, rx - dx
            within = 0 <= ky < 3 and 0 <= kx < 3
            blocks.append(weight[ky, kx, :, kt * CH : (kt + 1) * CH].astype(F32) if within else zero)
    row = (dy * 2 + dx) * CH
    w2[kt, row : row + CH, :] = jnp.concatenate(blocks, axis=1).astype(BF)


def gather_taps(in_weight, in_bias, taps):
    rest = in_bias[...]
    split = []
    for _ in range(3):
        part = rest.astype(BF).astype(F32)
        split.append(part)
        rest = rest - part
    rows = [in_weight[ky, i].astype(F32) for ky in range(3) for i in range(9)]
    taps[...] = jnp.transpose(jnp.concatenate(rows + split, axis=0)).astype(BF)


def lay_first(taps, spread, w1, ry):
    for pos in range(4 * ry, 4 * ry + 4):
        w1[pos * CH : (pos + 1) * CH, :] = lax.dot_general(
            taps[...], spread[:, pos * 384 : (pos + 1) * 384], NN, preferred_element_type=F32
        ).astype(BF)


SUBS = 2
PLAN_A = 64
LAG = 12
PACE = 1


def gather_kernel(
    clip_hbm,
    slab_hbm,
    pix,
    tok_hbm,
    perm_hbm,
    pick_hbm,
    spread_hbm,
    in_weight_hbm,
    in_bias_hbm,
    gain_hbm,
    weight_hbm,
    bias_hbm,
    out,
    words,
    entry,
    scales,
    w1,
    w2,
    clip_s,
    slab,
    mine_v,
    tok,
    perm,
    pick,
    spread,
    in_weight,
    in_bias,
    gain,
    weight,
    bias,
    load_sem,
    taps,
    own,
    edge,
    total,
    s0,
    r0,
    s1,
    r1,
    keep,
    s2,
    r2,
    s3,
    r3,
    s4,
    r4,
):
    w = lax.axis_index("wide")
    n = lax.axis_index("narrow")
    z, y = w // RING, w % RING
    x, c = n // 2, n % 2
    sibling = (w, x * 2 + 1 - c)
    near = x + 2 * c - 1
    near_ok = jnp.logical_and(near >= 0, near <= 3)
    major = (z, y)
    minor = (y, z)

    def wide_of(piece, maj, mnr):
        return maj * RING + mnr if piece == 0 else mnr * RING + maj

    def along_minor(piece, d):
        return (wide_of(piece, major[piece], (minor[piece] + d) % RING), n)

    def along_major(piece, d):
        return (wide_of(piece, (major[piece] + d) % RING, minor[piece]), n)

    pairs = [
        (pix.at[pl.ds(2 * c, 2)], mine_v),
        (perm_hbm, perm),
        (pick_hbm, pick),
        (tok_hbm, tok),
        (spread_hbm.at[c], spread),
        (in_weight_hbm, in_weight),
        (in_bias_hbm, in_bias),
        (weight_hbm, weight),
        (clip_hbm, clip_s),
        (slab_hbm, slab),
        (gain_hbm, gain),
        (bias_hbm, bias),
    ]
    loads = [pltpu.make_async_copy(src, dst, load_sem.at[i]) for i, (src, dst) in enumerate(pairs)]
    for copy in loads:
        copy.start()

    barrier = pltpu.get_barrier_semaphore()
    pl.semaphore_signal(barrier, inc=1, device_id=sibling, device_id_type=MESH)
    for piece in range(2):
        for d in range(1, RING):
            pl.semaphore_signal(barrier, inc=1, device_id=along_minor(piece, d), device_id_type=MESH)

    for side in (1, 3):
        for core in range(2):
            beside = ((x + side) % 4) * 2 + core
            pl.semaphore_signal(barrier, inc=1, device_id=(w, beside), device_id_type=MESH)
    pl.semaphore_wait(barrier, 19)

    def to_sibling():
        return pltpu.make_async_remote_copy(
            pix.at[pl.ds(2 * (1 - c), 2)], edge.at[0], s0.at[0], r0.at[0], sibling, MESH
        )

    def to_near(core):
        return pltpu.make_async_remote_copy(
            pix.at[pl.ds(2 * core, 2)],
            edge.at[2 - c],
            s0.at[1 + core],
            r0.at[2 - c],
            (w, jnp.clip(near, 0, 3) * 2 + core),
            MESH,
        )

    def arrival(region):
        return pltpu.make_async_remote_copy(
            pix.at[pl.ds(0, 2)], edge.at[region], s0.at[0], r0.at[region], sibling, MESH
        )

    to_sibling().start()

    @pl.when(near_ok)
    def _():
        to_near(0).start()
        to_near(1).start()

    @pl.when(x == 0)
    def _():
        edge[1] = jnp.zeros_like(edge[1])

    @pl.when(x == 3)
    def _():
        edge[2] = jnp.zeros_like(edge[2])

    arrival(0).wait_recv()

    @pl.when(x > 0)
    def _():
        arrival(1).wait_recv()

    @pl.when(x < 3)
    def _():
        arrival(2).wait_recv()

    for copy in loads[:3]:
        copy.wait()
    for piece in range(2):
        mine = mine_v[piece].astype(F32).reshape(24, 128)
        other = edge[0, piece].astype(F32).reshape(24, 128)
        low = edge[1, piece].astype(F32).reshape(24, 128)
        high = edge[2, piece].astype(F32).reshape(24, 128)
        first = jnp.where(c == 0, mine, other)
        second = jnp.where(c == 0, other, mine)
        stack = jnp.concatenate([low, first, second, high], axis=0).astype(BF)
        laid = lax.dot_general(perm[...], stack, NN, preferred_element_type=F32).astype(BF)
        rows = lax.dot_general(pick[0], laid[:128], NT, preferred_element_type=F32)
        rows += lax.dot_general(pick[1], laid[128:], NT, preferred_element_type=F32)
        own[piece] = rows.astype(BF)

    def local(piece):
        return pltpu.make_async_copy(own.at[piece], out.at[piece, c, major[piece], minor[piece]], keep.at[piece])

    def first_hop(piece, d, slot):
        return pltpu.make_async_remote_copy(
            own.at[piece],
            out.at[piece, c, major[piece], slot],
            s1.at[piece, d],
            r1.at[piece, d],
            along_minor(piece, d),
            MESH,
        )

    order = (4, 3, 5, 2, 6, 1, 7)
    for piece in range(2):
        for d in order:
            first_hop(piece, d, minor[piece]).start()
    for piece in range(2):
        local(piece).start()

    for copy in loads[3:]:
        copy.wait()
    total[...] = jnp.zeros_like(total)
    plan_steps(tok, total, w * TOK, 0, PLAN_A)

    def last_words():
        plan_words(total, clip_starts(clip_s), words, entry)
        words[24:26, :] = slab[...]
        scales[0:1, 0:CH] = gain[...]
        scales[1:2, 0:CH] = bias[...]

    work = [
        functools.partial(plan_steps, tok, total, w * TOK, q, q + 8) for q in range(PLAN_A, TOK * 64 // PLAN, 8)
    ]
    work += [functools.partial(gather_taps, in_weight, in_bias, taps), last_words]
    work += [functools.partial(lay_first, taps, spread, w1, ry) for ry in range(4)]
    work += [
        functools.partial(lay_second, weight, w2, kt, dy, dx)
        for kt in range(3)
        for dy in range(2)
        for dx in range(2)
    ]

    part = RING // SUBS

    def hop(piece, way, k, h, arrived):
        step = 1 - 2 * way
        chunk = (major[piece] - step * (k if arrived else k - 1)) % RING
        ref = out.at[piece, c, chunk, pl.ds(part * h, part)]
        return pltpu.make_async_remote_copy(
            ref, ref, s2.at[piece, way, k - 1, h], r2.at[piece, way, k - 1, h], along_major(piece, step), MESH
        )

    def share(piece, way, k, h, core):
        chunk = (major[piece] - (1 - 2 * way) * k) % RING
        where = (piece, core, chunk, pl.ds(part * h, part))
        return pltpu.make_async_remote_copy(
            out.at[where], out.at[where], s3.at[piece, way, k - 1, h], r3.at[piece, way, k - 1, h], sibling, MESH
        )

    def share_own(piece, core):
        where = (piece, core, major[piece])
        return pltpu.make_async_remote_copy(out.at[where], out.at[where], s4.at[piece], r4.at[piece], sibling, MESH)

    def turned(way, i):
        return i if way == 0 else SUBS - 1 - i

    for piece in range(2):
        local(piece).wait()
        for d in reversed(order):
            first_hop(piece, d, (minor[piece] - d) % RING).wait_recv()
        for i in range(SUBS):
            for way in range(2):
                hop(piece, way, 1, turned(way, i), False).start()
    for piece in range(2):
        share_own(piece, c).start()

    moves = []
    for k in range(1, 5):
        for i in range(SUBS):
            for piece in range(2):
                for way in range(2):
                    if k < 4 or i < SUBS // 2:
                        moves.append((piece, way, k, turned(way, i), k < 3 or (k == 3 and i < SUBS // 2)))
    to_sibling().wait_send()

    @pl.when(near_ok)
    def _():
        to_near(0).wait_send()
        to_near(1).wait_send()

    for at, (piece, way, k, h, onward) in enumerate(moves):
        hop(piece, way, k, h, True).wait_recv()
        if onward:
            hop(piece, way, k + 1, h, False).start()
        share(piece, way, k, h, c).start()
        if at < 14:
            first_hop(at % 2, order[at // 2], minor[at % 2]).wait_send()
        if at >= LAG:
            hop(*moves[at - LAG][:4], False).wait_send()
            share(*moves[at - LAG][:4], c).wait_send()
        for _ in range(PACE):
            if work:
                work.pop(0)()
    for task in work:
        task()

    for piece in range(2):
        share_own(piece, c).wait_send()
        share_own(piece, 1 - c).wait_recv()
    for at, (piece, way, k, h, onward) in enumerate(moves):
        if at >= len(moves) - LAG:
            hop(piece, way, k, h, False).wait_send()
            share(piece, way, k, h, c).wait_send()
        share(piece, way, k, h, 1 - c).wait_recv()


def gather_tables(clip_lengths, slab_place, pixel_slabs, tok_place, in_weight, in_bias, gain, weight, bias):
    perm, pick = placement_tables()
    dma = pltpu.SemaphoreType.DMA
    vmem = pl.BlockSpec(memory_space=pltpu.VMEM)
    shape = (2, 2, RING, RING, 64, 128)
    return pl.pallas_call(
        gather_kernel,
        out_shape=(
            jax.ShapeDtypeStruct(shape, BF),
            jax.ShapeDtypeStruct((32, 128), jnp.int32),
            jax.ShapeDtypeStruct((8, 128), jnp.int32),
            jax.ShapeDtypeStruct((8, 128), F32),
            jax.ShapeDtypeStruct((16 * CH, 384), BF),
            jax.ShapeDtypeStruct((3, 4 * CH, 16 * CH), BF),
        ),
        in_specs=[pl.BlockSpec(memory_space=pltpu.HBM)] * 12,
        out_specs=(pl.BlockSpec(memory_space=pl.ANY), vmem, vmem, vmem, vmem, vmem),
        scratch_shapes=[
            pltpu.SMEM((6,), jnp.int32),
            pltpu.VMEM((2, 128), jnp.int32),
            pltpu.VMEM((2, 3, 8, 128), BF),
            pltpu.VMEM((512, 128), jnp.int32),
            pltpu.VMEM((256, 96), BF),
            pltpu.VMEM((2, 64, 128), BF),
            pltpu.VMEM((84, 16 * 384), BF),
            pltpu.VMEM((3, 9, 3, CH), BF),
            pltpu.VMEM((1, CH), F32),
            pltpu.VMEM((1, CH), F32),
            pltpu.VMEM((3, 3, CH, 3 * CH), BF),
            pltpu.VMEM((1, CH), F32),
            dma((12,)),
            pltpu.VMEM((CH, 84), BF),
            pltpu.VMEM((2, 64, 128), BF),
            pltpu.VMEM((3, 2, 3, 8, 128), BF),
            pltpu.VMEM((64, 32), F32),
            dma((3,)),
            dma((3,)),
            dma((2, RING)),
            dma((2, RING)),
            dma((2,)),
            dma((2, 2, 4, SUBS)),
            dma((2, 2, 4, SUBS)),
            dma((2, 2, 4, SUBS)),
            dma((2, 2, 4, SUBS)),
            dma((2,)),
            dma((2,)),
        ],
        compiler_params=pltpu.CompilerParams(
            collective_id=0, has_side_effects=True, vmem_limit_bytes=16 << 20
        ),
        name="gather_tables",
    )(
        *[pltpu.with_memory_space_constraint(v, pltpu.HBM) for v in (
        clip_lengths,
        slab_place.reshape(2, 128),
        pixel_slabs,
        tok_place.reshape(512, 128),
        jnp.asarray(perm, BF),
        jnp.asarray(pick, BF),
        jnp.asarray(weight_table(), BF),
        jnp.transpose(in_weight, (0, 3, 1, 2)),
        in_bias.reshape(1, CH),
        gain.reshape(1, CH),
        weight,
        bias.reshape(1, CH),
        )]
    )


TILE = 1024
BATCH = 32


def column(row):
    n = row.shape[1]
    same = lax.broadcasted_iota(jnp.int32, (n, n), 0) == lax.broadcasted_iota(jnp.int32, (n, n), 1)
    return jnp.sum(jnp.where(same, jnp.broadcast_to(row, (n, n)), 0.0), axis=1, keepdims=True)


def main_kernel(words, entry, least, table, scales, w1, w2, out, frames, patches, shifts, hid, act):
    n = lax.axis_index("narrow")
    c = n % 2

    half_gain = column(scales[0:1, 0:CH]) * 0.5
    out_bias = column(scales[1:2, 0:CH])
    lane = lax.broadcasted_iota(jnp.int32, (8, 128), 1)
    for j in range(4):
        shifts[8 * j : 8 * j + 8, :] = (lane + 256 - (48 * c + 12 * j)) & 127

    frames[0 : LEAD * FRAME_ROWS, :] = jnp.zeros((LEAD * FRAME_ROWS, 128), F32)
    frames[(LEAD + 256) * FRAME_ROWS : (LEAD + 256) * FRAME_ROWS + 8, :] = jnp.zeros((8, 128), F32)
    for k in range(8):
        piece, core = k // 4, (k // 2) % 2

        def fill(m, carry):
            maj = (k % 2) * 4 + m
            at = []
            for mnr in range(RING):
                wide = maj * RING + mnr if piece == 0 else mnr * RING + maj
                frame = words[3 * TOK + wide * 4 + core * 2 + piece]
                at.append(pl.multiple_of((frame + LEAD) * FRAME_ROWS, 8))
            for mnr in range(RING):
                frames[pl.ds(at[mnr], 8), :] = jnp.zeros((8, 128), F32)
                frames[pl.ds(at[mnr] + 8, 64), :] = table[32 * k + m * RING + mnr].astype(F32)
            return carry

        lax.fori_loop(0, 4, fill, 0)

    late = lax.broadcasted_iota(jnp.int32, (5, 128), 0)

    def pick_up(s):
        base, j, oldest = words[s], words[TOK + s], words[2 * TOK + s]
        rel = shifts[pl.ds(pl.multiple_of(j * 8, 8), 5), :]
        left = frames[pl.ds(base, 5, stride=FRAME_ROWS), :]
        mid = pltpu.roll(frames[pl.ds(base + 1, 5, stride=FRAME_ROWS), :], 36, 1)
        right = pltpu.roll(frames[pl.ds(base + 2, 5, stride=FRAME_ROWS), :], 72, 1)
        row = jnp.where(rel < 36, left, jnp.where(rel < 72, mid, jnp.where(rel < 108, right, 1.0)))
        row = jnp.where(late >= oldest, row, 0.0)
        return pltpu.roll(row, 128 - 12 * j, 1)

    def pull(q, carry):
        rows = [pick_up(q * BATCH + i) for i in range(BATCH)]
        for i in range(BATCH):
            patches[pl.ds(q * BATCH + i, 5, stride=TOK), :] = rows[i]
        return carry

    lax.fori_loop(0, TOK // BATCH, pull, 0)

    def tile(g, carry):
        at = pl.multiple_of(g * TILE, TILE)
        e, old = [
            jnp.concatenate([ref[pl.ds(g * (TILE // 128) + i, 1), :] for i in range(TILE // 128)], axis=1)
            for ref in (entry, least.at[pl.ds(16, 8)])
        ]
        j, col, age = (e >> 6) & 3, e & 63, 4 - old
        row_ok = [
            jnp.logical_not(jnp.logical_and(j == 0, n == 0)),
            None,
            None,
            jnp.logical_not(jnp.logical_and(j == 3, n == 7)),
        ]
        col_ok = [col != 0, None, None, col != 63]
        total = jnp.concatenate([jnp.broadcast_to(out_bias, (CH, TILE))] * 4, axis=0)
        for s in range(3):
            block = jnp.concatenate(
                [patches[pl.ds(pl.multiple_of((s + kt) * TOK + at, TILE), TILE), :].astype(BF) for kt in range(3)],
                axis=1,
            )
            hid[...] = lax.dot_general(w1[...], block, NT, preferred_element_type=F32)
            for ry in range(4):
                for rx in range(4):
                    pos = ry * 4 + rx
                    h = hid[pos * CH : (pos + 1) * CH, :]
                    scale = lax.rsqrt(jnp.sum(h * h, axis=0, keepdims=True) * (1.0 / CH) + EPSILON)
                    ok = age >= 2 - s
                    if row_ok[ry] is not None:
                        ok = jnp.logical_and(ok, row_ok[ry])
                    if col_ok[rx] is not None:
                        ok = jnp.logical_and(ok, col_ok[rx])
                    u = h * jnp.where(ok, scale, 0.0) * half_gain
                    act[pos * CH : (pos + 1) * CH, :] = (u + u * jnp.tanh(u)).astype(BF)
            total = total + lax.dot_general(w2[s], act[...], NN, preferred_element_type=F32)
            if s == 2:
                keep = [hid[(ry * 4 + rx) * CH : (ry * 4 + rx + 1) * CH, :] for ry in (1, 2) for rx in (1, 2)]
                total = total + jnp.concatenate(keep, axis=0)
        out[pl.ds(at, TILE), :] = jnp.transpose(total).astype(BF)
        return carry

    lax.fori_loop(0, TOK // TILE, tile, 0)


def encode(words, entry, table, scales, w1, w2):
    vmem = pl.BlockSpec(memory_space=pltpu.VMEM)
    return pl.pallas_call(
        main_kernel,
        out_shape=jax.ShapeDtypeStruct((TOK, 4 * CH), BF),
        in_specs=[pl.BlockSpec(memory_space=pltpu.SMEM)] + [vmem] * 6,
        out_specs=vmem,
        scratch_shapes=[
            pltpu.VMEM(((LEAD + 256) * FRAME_ROWS + 8, 128), F32),
            pltpu.VMEM((5 * TOK, 128), F32),
            pltpu.VMEM((32, 128), jnp.int32),
            pltpu.VMEM((16 * CH, TILE), F32),
            pltpu.VMEM((16 * CH, TILE), BF),
        ],
        compiler_params=pltpu.CompilerParams(vmem_limit_bytes=42 << 20),
        name="encode",
    )(words.reshape(4 * TOK), entry, words, table.reshape(256, 64, 128), scales, w1, w2)


def body(
    pixel_slabs,
    conv_in_weight,
    conv_in_bias,
    norm_gain,
    conv_weight,
    conv_bias,
    clip_lengths,
    slab_place,
    tok_place,
):
    table, words, entry, scales, w1, w2 = gather_tables(
        clip_lengths,
        slab_place,
        pixel_slabs,
        tok_place,
        conv_in_weight,
        conv_in_bias,
        norm_gain,
        conv_weight,
        conv_bias,
    )
    return encode(words, entry, table, scales, w1, w2)


def solution(mesh):
    placed = (P("wide", None, "narrow", None), P(), P(), P(), P(), P(), P(), P(), P())
    return jax.shard_map(
        body, mesh=mesh, in_specs=placed, out_specs=P(("wide", "narrow"), None), check_vma=False
    )
```

```python
import functools

import jax
import jax.numpy as jnp
import numpy as np
from jax import lax
from jax.experimental import pallas as pl
from jax.experimental.pallas import tpu as pltpu
from jax.sharding import PartitionSpec as P

EPSILON = 1e-06
MESH = pl.DeviceIdType.MESH
BF = jnp.bfloat16
F32 = jnp.float32
RING = 8
CH = 96
TOK = 1024
FRAME_ROWS = 72
LEAD = 4
NT = (((1,), (1,)), ((), ()))
NN = (((1,), (0,)), ((), ()))


def placement_tables():
    perm = np.zeros((256, 96), np.float32)
    for row in range(20):
        region, inner = (0, 6 + row) if row < 2 else ((1, row - 2) if row < 10 else ((2, row - 10) if row < 18 else (3, row - 18)))
        for parity in range(2):
            for ch in range(3):
                perm[parity * 128 + row * 6 + parity * 3 + ch, region * 24 + ch * 8 + inner] = 1
    pick = np.zeros((2, 64, 128), np.float32)
    for parity in range(2):
        for pair in range(64):
            pick[parity, pair, 2 * pair + parity] = 1
    return perm, pick


def slot_of(ry, rx):
    return (rx // 2) * 8 + ry * 2 + rx % 2


def weight_table():
    table = np.zeros((84, 16 * 256), np.float32)
    for ry in range(4):
        for rx in range(4):
            base = slot_of(ry, rx) * 256
            for ky in range(3):
                for kx in range(3):
                    for kt in range(3):
                        for ch in range(3):
                            row, col = ry + ky, rx + kx
                            lane = (col // 2 - rx // 2) * 36 + row * 6 + (col % 2) * 3 + ch
                            table[(ky * 9 + kt * 3 + ch) * 3 + kx, base + kt * 72 + lane] = 1
            for part in range(3):
                table[81 + part, base + 216 + part] = 1
    return table


def clip_age(starts, t):
    latest = jnp.zeros_like(t)
    for i in range(1, 6):
        latest = jnp.where(starts[i] <= t, starts[i], latest)
    return t - latest


def clip_starts(clip_s):
    starts = [jnp.int32(0)]
    for i in range(5):
        starts.append(starts[-1] + clip_s[i])
    return starts


PLAN = 1024


def plan_steps(tok, total, base, first, last):
    sub = lax.broadcasted_iota(jnp.int32, (32, PLAN), 0)
    high_of = ((sub % 8) * 4 + sub // 8).astype(F32).astype(BF)
    low_of = sub.astype(F32).astype(BF)
    lane = lax.broadcasted_iota(jnp.int32, (32, PLAN), 1)
    inside = (lane % 256).astype(F32).astype(BF)
    frame = (lane // 256).astype(F32)
    none = jnp.zeros((32, PLAN), BF)
    ones = jnp.ones((32, PLAN), BF)

    def spread_rows(rows):
        wide = [jnp.broadcast_to(rows[i : i + 1], (32, 128)).astype(BF) for i in range(8)]
        return jnp.concatenate(wide, axis=1)

    def step(q, carry):
        rows = tok[pl.ds(pl.multiple_of(q * 8, 8), 8), :] - base
        high = spread_rows(jnp.clip(rows >> 5, -1, 64).astype(F32))
        low = spread_rows((rows & 31).astype(F32))
        hit = high == high_of
        times = jnp.where(hit, (frame + (q * (PLAN // 256)).astype(F32)).astype(BF), none)
        left = jnp.concatenate([times, jnp.where(hit, inside, none)], axis=0)
        right = jnp.where(low == low_of, ones, none)
        total[...] += lax.dot_general(left, right, NT, preferred_element_type=F32)
        return carry

    lax.fori_loop(first, last, step, 0, unroll=4)


def plan_words(total, starts, words, entry):
    found = (total[:32, :] * 256.0 + total[32:, :]).astype(jnp.int32)
    e = jnp.concatenate([found[8 * m : 8 * m + 8] for m in range(4)], axis=1)
    entry[...] = e
    t, j, col = e >> 8, (e >> 6) & 3, e & 63
    words[0:8, :] = t * FRAME_ROWS + 7 + col
    words[8:16, :] = j
    words[16:24, :] = 4 - clip_age(starts, t)


def lay_second(weight, w2, kt, dy, dx):
    zero = jnp.zeros((CH, CH), F32)
    blocks = []
    for ry in range(4):
        for rx in range(4):
            ky, kx = ry - dy, rx - dx
            within = 0 <= ky < 3 and 0 <= kx < 3
            blocks.append(weight[ky, kx, :, kt * CH : (kt + 1) * CH].astype(F32) if within else zero)
    row = (dy * 2 + dx) * CH
    w2[kt, row : row + CH, :] = jnp.concatenate(blocks, axis=1).astype(BF)


def gather_taps(in_weight, in_bias, taps):
    rest = in_bias[...]
    split = []
    for _ in range(3):
        part = rest.astype(BF).astype(F32)
        split.append(part)
        rest = rest - part
    rows = [in_weight[ky, i].astype(F32) for ky in range(3) for i in range(9)]
    taps[...] = jnp.transpose(jnp.concatenate(rows + split, axis=0)).astype(BF)


def lay_first(taps, spread, w1, ry):
    for pos in range(4 * ry, 4 * ry + 4):
        w1[pos * CH : (pos + 1) * CH, :] = lax.dot_general(
            taps[...], spread[:, pos * 256 : (pos + 1) * 256], NN, preferred_element_type=F32
        ).astype(BF)


SUBS = 2
PLAN_A = 64
LAG = 12
PACE = 1


def gather_kernel(
    clip_hbm,
    slab_hbm,
    pix,
    tok_hbm,
    perm_hbm,
    pick_hbm,
    spread_hbm,
    in_weight_hbm,
    in_bias_hbm,
    gain_hbm,
    weight_hbm,
    bias_hbm,
    out,
    words,
    entry,
    scales,
    w1,
    w2,
    clip_s,
    slab,
    mine_v,
    tok,
    perm,
    pick,
    spread,
    in_weight,
    in_bias,
    gain,
    weight,
    bias,
    load_sem,
    taps,
    own,
    edge,
    total,
    s0,
    r0,
    s1,
    r1,
    keep,
    s2,
    r2,
    s3,
    r3,
    s4,
    r4,
):
    w = lax.axis_index("wide")
    n = lax.axis_index("narrow")
    z, y = w // RING, w % RING
    x, c = n // 2, n % 2
    sibling = (w, x * 2 + 1 - c)
    near = x + 2 * c - 1
    near_ok = jnp.logical_and(near >= 0, near <= 3)
    major = (z, y)
    minor = (y, z)

    def wide_of(piece, maj, mnr):
        return maj * RING + mnr if piece == 0 else mnr * RING + maj

    def along_minor(piece, d):
        return (wide_of(piece, major[piece], (minor[piece] + d) % RING), n)

    def along_major(piece, d):
        return (wide_of(piece, (major[piece] + d) % RING, minor[piece]), n)

    pairs = [
        (pix.at[pl.ds(2 * c, 2)], mine_v),
        (perm_hbm, perm),
        (pick_hbm, pick),
        (tok_hbm, tok),
        (spread_hbm, spread),
        (in_weight_hbm, in_weight),
        (in_bias_hbm, in_bias),
        (weight_hbm, weight),
        (clip_hbm, clip_s),
        (slab_hbm, slab),
        (gain_hbm, gain),
        (bias_hbm, bias),
    ]
    loads = [pltpu.make_async_copy(src, dst, load_sem.at[i]) for i, (src, dst) in enumerate(pairs)]
    for copy in loads:
        copy.start()

    barrier = pltpu.get_barrier_semaphore()
    pl.semaphore_signal(barrier, inc=1, device_id=sibling, device_id_type=MESH)
    for piece in range(2):
        for d in range(1, RING):
            pl.semaphore_signal(barrier, inc=1, device_id=along_minor(piece, d), device_id_type=MESH)

    for side in (1, 3):
        for core in range(2):
            beside = ((x + side) % 4) * 2 + core
            pl.semaphore_signal(barrier, inc=1, device_id=(w, beside), device_id_type=MESH)
    pl.semaphore_wait(barrier, 19)

    def to_sibling():
        return pltpu.make_async_remote_copy(
            pix.at[pl.ds(2 * (1 - c), 2)], edge.at[0], s0.at[0], r0.at[0], sibling, MESH
        )

    def to_near(core):
        return pltpu.make_async_remote_copy(
            pix.at[pl.ds(2 * core, 2)],
            edge.at[2 - c],
            s0.at[1 + core],
            r0.at[2 - c],
            (w, jnp.clip(near, 0, 3) * 2 + core),
            MESH,
        )

    def arrival(region):
        return pltpu.make_async_remote_copy(
            pix.at[pl.ds(0, 2)], edge.at[region], s0.at[0], r0.at[region], sibling, MESH
        )

    to_sibling().start()

    @pl.when(near_ok)
    def _():
        to_near(0).start()
        to_near(1).start()

    @pl.when(x == 0)
    def _():
        edge[1] = jnp.zeros_like(edge[1])

    @pl.when(x == 3)
    def _():
        edge[2] = jnp.zeros_like(edge[2])

    arrival(0).wait_recv()

    @pl.when(x > 0)
    def _():
        arrival(1).wait_recv()

    @pl.when(x < 3)
    def _():
        arrival(2).wait_recv()

    for copy in loads[:3]:
        copy.wait()
    for piece in range(2):
        mine = mine_v[piece].astype(F32).reshape(24, 128)
        other = edge[0, piece].astype(F32).reshape(24, 128)
        low = edge[1, piece].astype(F32).reshape(24, 128)
        high = edge[2, piece].astype(F32).reshape(24, 128)
        first = jnp.where(c == 0, mine, other)
        second = jnp.where(c == 0, other, mine)
        stack = jnp.concatenate([low, first, second, high], axis=0).astype(BF)
        laid = lax.dot_general(perm[...], stack, NN, preferred_element_type=F32).astype(BF)
        rows = lax.dot_general(pick[0], laid[:128], NT, preferred_element_type=F32)
        rows += lax.dot_general(pick[1], laid[128:], NT, preferred_element_type=F32)
        own[piece] = rows.astype(BF)

    def local(piece):
        return pltpu.make_async_copy(own.at[piece], out.at[piece, c, major[piece], minor[piece]], keep.at[piece])

    def first_hop(piece, d, slot):
        return pltpu.make_async_remote_copy(
            own.at[piece],
            out.at[piece, c, major[piece], slot],
            s1.at[piece, d],
            r1.at[piece, d],
            along_minor(piece, d),
            MESH,
        )

    order = (4, 3, 5, 2, 6, 1, 7)
    for piece in range(2):
        for d in order:
            first_hop(piece, d, minor[piece]).start()
    for piece in range(2):
        local(piece).start()

    for copy in loads[3:]:
        copy.wait()
    total[...] = jnp.zeros_like(total)
    plan_steps(tok, total, w * TOK, 0, PLAN_A)

    def last_words():
        plan_words(total, clip_starts(clip_s), words, entry)
        words[24:26, :] = slab[...]
        scales[0:1, 0:CH] = gain[...]
        scales[1:2, 0:CH] = bias[...]

    work = [
        functools.partial(plan_steps, tok, total, w * TOK, q, q + 8) for q in range(PLAN_A, TOK * 64 // PLAN, 8)
    ]
    work += [functools.partial(gather_taps, in_weight, in_bias, taps), last_words]
    work += [functools.partial(lay_first, taps, spread, w1, ry) for ry in range(4)]
    work += [
        functools.partial(lay_second, weight, w2, kt, dy, dx)
        for kt in range(3)
        for dy in range(2)
        for dx in range(2)
    ]

    part = RING // SUBS

    def hop(piece, way, k, h, arrived):
        step = 1 - 2 * way
        chunk = (major[piece] - step * (k if arrived else k - 1)) % RING
        ref = out.at[piece, c, chunk, pl.ds(part * h, part)]
        return pltpu.make_async_remote_copy(
            ref, ref, s2.at[piece, way, k - 1, h], r2.at[piece, way, k - 1, h], along_major(piece, step), MESH
        )

    def share(piece, way, k, h, core):
        chunk = (major[piece] - (1 - 2 * way) * k) % RING
        where = (piece, core, chunk, pl.ds(part * h, part))
        return pltpu.make_async_remote_copy(
            out.at[where], out.at[where], s3.at[piece, way, k - 1, h], r3.at[piece, way, k - 1, h], sibling, MESH
        )

    def share_own(piece, core):
        where = (piece, core, major[piece])
        return pltpu.make_async_remote_copy(out.at[where], out.at[where], s4.at[piece], r4.at[piece], sibling, MESH)

    def turned(way, i):
        return i if way == 0 else SUBS - 1 - i

    for piece in range(2):
        local(piece).wait()
        for d in reversed(order):
            first_hop(piece, d, (minor[piece] - d) % RING).wait_recv()
        for i in range(SUBS):
            for way in range(2):
                hop(piece, way, 1, turned(way, i), False).start()
    for piece in range(2):
        share_own(piece, c).start()

    moves = []
    for k in range(1, 5):
        for i in range(SUBS):
            for piece in range(2):
                for way in range(2):
                    if k < 4 or i < SUBS // 2:
                        moves.append((piece, way, k, turned(way, i), k < 3 or (k == 3 and i < SUBS // 2)))
    to_sibling().wait_send()

    @pl.when(near_ok)
    def _():
        to_near(0).wait_send()
        to_near(1).wait_send()

    for at, (piece, way, k, h, onward) in enumerate(moves):
        hop(piece, way, k, h, True).wait_recv()
        if onward:
            hop(piece, way, k + 1, h, False).start()
        share(piece, way, k, h, c).start()
        if at < 14:
            first_hop(at % 2, order[at // 2], minor[at % 2]).wait_send()
        if at >= LAG:
            hop(*moves[at - LAG][:4], False).wait_send()
            share(*moves[at - LAG][:4], c).wait_send()
        for _ in range(PACE):
            if work:
                work.pop(0)()
    for task in work:
        task()

    for piece in range(2):
        share_own(piece, c).wait_send()
        share_own(piece, 1 - c).wait_recv()
    for at, (piece, way, k, h, onward) in enumerate(moves):
        if at >= len(moves) - LAG:
            hop(piece, way, k, h, False).wait_send()
            share(piece, way, k, h, c).wait_send()
        share(piece, way, k, h, 1 - c).wait_recv()


def gather_tables(clip_lengths, slab_place, pixel_slabs, tok_place, in_weight, in_bias, gain, weight, bias):
    perm, pick = placement_tables()
    dma = pltpu.SemaphoreType.DMA
    vmem = pl.BlockSpec(memory_space=pltpu.VMEM)
    shape = (2, 2, RING, RING, 64, 128)
    return pl.pallas_call(
        gather_kernel,
        out_shape=(
            jax.ShapeDtypeStruct(shape, BF),
            jax.ShapeDtypeStruct((32, 128), jnp.int32),
            jax.ShapeDtypeStruct((8, 128), jnp.int32),
            jax.ShapeDtypeStruct((8, 128), F32),
            jax.ShapeDtypeStruct((16 * CH, 256), BF),
            jax.ShapeDtypeStruct((3, 4 * CH, 16 * CH), BF),
        ),
        in_specs=[pl.BlockSpec(memory_space=pltpu.HBM)] * 12,
        out_specs=(pl.BlockSpec(memory_space=pl.ANY), vmem, vmem, vmem, vmem, vmem),
        scratch_shapes=[
            pltpu.SMEM((6,), jnp.int32),
            pltpu.VMEM((2, 128), jnp.int32),
            pltpu.VMEM((2, 3, 8, 128), BF),
            pltpu.VMEM((512, 128), jnp.int32),
            pltpu.VMEM((256, 96), BF),
            pltpu.VMEM((2, 64, 128), BF),
            pltpu.VMEM((84, 16 * 256), BF),
            pltpu.VMEM((3, 9, 3, CH), BF),
            pltpu.VMEM((1, CH), F32),
            pltpu.VMEM((1, CH), F32),
            pltpu.VMEM((3, 3, CH, 3 * CH), BF),
            pltpu.VMEM((1, CH), F32),
            dma((12,)),
            pltpu.VMEM((CH, 84), BF),
            pltpu.VMEM((2, 64, 128), BF),
            pltpu.VMEM((3, 2, 3, 8, 128), BF),
            pltpu.VMEM((64, 32), F32),
            dma((3,)),
            dma((3,)),
            dma((2, RING)),
            dma((2, RING)),
            dma((2,)),
            dma((2, 2, 4, SUBS)),
            dma((2, 2, 4, SUBS)),
            dma((2, 2, 4, SUBS)),
            dma((2, 2, 4, SUBS)),
            dma((2,)),
            dma((2,)),
        ],
        compiler_params=pltpu.CompilerParams(
            collective_id=0, has_side_effects=True, vmem_limit_bytes=16 << 20
        ),
        name="gather_tables",
    )(
        *[pltpu.with_memory_space_constraint(v, pltpu.HBM) for v in (
        clip_lengths,
        slab_place.reshape(2, 128),
        pixel_slabs,
        tok_place.reshape(512, 128),
        jnp.asarray(perm, BF),
        jnp.asarray(pick, BF),
        jnp.asarray(weight_table(), BF),
        jnp.transpose(in_weight, (0, 3, 1, 2)),
        in_bias.reshape(1, CH),
        gain.reshape(1, CH),
        weight,
        bias.reshape(1, CH),
        )]
    )


TILE = 1024
BATCH = 32


def column(row):
    n = row.shape[1]
    same = lax.broadcasted_iota(jnp.int32, (n, n), 0) == lax.broadcasted_iota(jnp.int32, (n, n), 1)
    return jnp.sum(jnp.where(same, jnp.broadcast_to(row, (n, n)), 0.0), axis=1, keepdims=True)


def main_kernel(words, entry, least, table, scales, w1, w2, out, frames, patches, shifts, hid, act):
    n = lax.axis_index("narrow")
    c = n % 2

    half_gain = column(scales[0:1, 0:CH]) * 0.5
    out_bias = column(scales[1:2, 0:CH])
    lane = lax.broadcasted_iota(jnp.int32, (8, 128), 1)
    for j in range(4):
        shifts[8 * j : 8 * j + 8, :] = (lane + 256 - (48 * c + 12 * j)) & 127

    frames[0 : LEAD * FRAME_ROWS, :] = jnp.zeros((LEAD * FRAME_ROWS, 128), F32)
    frames[(LEAD + 256) * FRAME_ROWS : (LEAD + 256) * FRAME_ROWS + 8, :] = jnp.zeros((8, 128), F32)
    for k in range(8):
        piece, core = k // 4, (k // 2) % 2

        def fill(m, carry):
            maj = (k % 2) * 4 + m
            at = []
            for mnr in range(RING):
                wide = maj * RING + mnr if piece == 0 else mnr * RING + maj
                frame = words[3 * TOK + wide * 4 + core * 2 + piece]
                at.append(pl.multiple_of((frame + LEAD) * FRAME_ROWS, 8))
            for mnr in range(RING):
                frames[pl.ds(at[mnr], 8), :] = jnp.zeros((8, 128), F32)
                frames[pl.ds(at[mnr] + 8, 64), :] = table[32 * k + m * RING + mnr].astype(F32)
            return carry

        lax.fori_loop(0, 4, fill, 0)

    late = lax.broadcasted_iota(jnp.int32, (5, 128), 0)

    def pick_up(s):
        base, j, oldest = words[s], words[TOK + s], words[2 * TOK + s]
        rel = shifts[pl.ds(pl.multiple_of(j * 8, 8), 5), :]
        left = frames[pl.ds(base, 5, stride=FRAME_ROWS), :]
        mid = pltpu.roll(frames[pl.ds(base + 1, 5, stride=FRAME_ROWS), :], 36, 1)
        right = pltpu.roll(frames[pl.ds(base + 2, 5, stride=FRAME_ROWS), :], 72, 1)
        row = jnp.where(rel < 36, left, jnp.where(rel < 72, mid, jnp.where(rel < 108, right, 1.0)))
        row = jnp.where(late >= oldest, row, 0.0)
        return pltpu.roll(row, (256 - 48 * c - 12 * j) & 127, 1)

    def pull(q, carry):
        rows = [pick_up(q * BATCH + i) for i in range(BATCH)]
        for i in range(BATCH):
            patches[pl.ds(q * BATCH + i, 5, stride=TOK), :] = rows[i]
        return carry

    lax.fori_loop(0, TOK // BATCH, pull, 0)

    def tile(g, carry):
        at = pl.multiple_of(g * TILE, TILE)
        e, old = [
            jnp.concatenate([ref[pl.ds(g * (TILE // 128) + i, 1), :] for i in range(TILE // 128)], axis=1)
            for ref in (entry, least.at[pl.ds(16, 8)])
        ]
        j, col, age = (e >> 6) & 3, e & 63, 4 - old
        row_ok = [
            jnp.logical_not(jnp.logical_and(j == 0, n == 0)),
            None,
            None,
            jnp.logical_not(jnp.logical_and(j == 3, n == 7)),
        ]
        col_ok = [col != 0, None, None, col != 63]
        spot = lax.broadcasted_iota(jnp.int32, (TILE, 128), 1)
        total = jnp.concatenate([jnp.broadcast_to(out_bias, (CH, TILE))] * 4, axis=0)
        for s in range(3):
            seen = [patches[pl.ds(pl.multiple_of((s + kt) * TOK + at, TILE), TILE), :] for kt in range(3)]
            for half in range(2):
                start = seen[0] if half == 0 else pltpu.roll(seen[0], 92, 1)
                middle = pltpu.roll(seen[1], 72 - 36 * half, 1)
                end = pltpu.roll(seen[2], 16 if half == 0 else 108, 1)
                left = jnp.where(spot < 72, start, middle).astype(BF)
                right = jnp.where(spot < 16, middle, jnp.where(spot < 88, end, 1.0)).astype(BF)
                rows = slice(half * 8 * CH, (half + 1) * 8 * CH)
                hid[rows, :] = lax.dot_general(
                    w1[rows, :], jnp.concatenate([left, right], axis=1), NT, preferred_element_type=F32
                )
            for ry in range(4):
                for rx in range(4):
                    pos = ry * 4 + rx
                    slot = slot_of(ry, rx) * CH
                    h = hid[slot : slot + CH, :]
                    scale = lax.rsqrt(jnp.sum(h * h, axis=0, keepdims=True) * (1.0 / CH) + EPSILON)
                    ok = age >= 2 - s
                    if row_ok[ry] is not None:
                        ok = jnp.logical_and(ok, row_ok[ry])
                    if col_ok[rx] is not None:
                        ok = jnp.logical_and(ok, col_ok[rx])
                    u = h * jnp.where(ok, scale, 0.0) * half_gain
                    act[pos * CH : (pos + 1) * CH, :] = (u + u * jnp.tanh(u)).astype(BF)
            total = total + lax.dot_general(w2[s], act[...], NN, preferred_element_type=F32)
            if s == 2:
                keep = [hid[slot_of(ry, rx) * CH : slot_of(ry, rx) * CH + CH, :] for ry in (1, 2) for rx in (1, 2)]
                total = total + jnp.concatenate(keep, axis=0)
        out[pl.ds(at, TILE), :] = jnp.transpose(total).astype(BF)
        return carry

    lax.fori_loop(0, TOK // TILE, tile, 0)


def encode(words, entry, table, scales, w1, w2):
    vmem = pl.BlockSpec(memory_space=pltpu.VMEM)
    return pl.pallas_call(
        main_kernel,
        out_shape=jax.ShapeDtypeStruct((TOK, 4 * CH), BF),
        in_specs=[pl.BlockSpec(memory_space=pltpu.SMEM)] + [vmem] * 6,
        out_specs=vmem,
        scratch_shapes=[
            pltpu.VMEM(((LEAD + 256) * FRAME_ROWS + 8, 128), F32),
            pltpu.VMEM((5 * TOK, 128), F32),
            pltpu.VMEM((32, 128), jnp.int32),
            pltpu.VMEM((16 * CH, TILE), F32),
            pltpu.VMEM((16 * CH, TILE), BF),
        ],
        compiler_params=pltpu.CompilerParams(vmem_limit_bytes=42 << 20),
        name="encode",
    )(words.reshape(4 * TOK), entry, words, table.reshape(256, 64, 128), scales, w1, w2)


def body(
    pixel_slabs,
    conv_in_weight,
    conv_in_bias,
    norm_gain,
    conv_weight,
    conv_bias,
    clip_lengths,
    slab_place,
    tok_place,
):
    table, words, entry, scales, w1, w2 = gather_tables(
        clip_lengths,
        slab_place,
        pixel_slabs,
        tok_place,
        conv_in_weight,
        conv_in_bias,
        norm_gain,
        conv_weight,
        conv_bias,
    )
    return encode(words, entry, table, scales, w1, w2)


def solution(mesh):
    placed = (P("wide", None, "narrow", None), P(), P(), P(), P(), P(), P(), P(), P())
    return jax.shard_map(
        body, mesh=mesh, in_specs=placed, out_specs=P(("wide", "narrow"), None), check_vma=False
    )
```

```python
import functools

import jax
import jax.numpy as jnp
import numpy as np
from jax import lax
from jax.experimental import pallas as pl
from jax.experimental.pallas import tpu as pltpu
from jax.sharding import PartitionSpec as P

EPSILON = 1e-06
MESH = pl.DeviceIdType.MESH
BF = jnp.bfloat16
F32 = jnp.float32
RING = 8
CH = 96
TOK = 1024
FRAME_ROWS = 72
LEAD = 4
NT = (((1,), (1,)), ((), ()))
NN = (((1,), (0,)), ((), ()))


def placement_tables():
    perm = np.zeros((256, 96), np.float32)
    for row in range(20):
        region, inner = (0, 6 + row) if row < 2 else ((1, row - 2) if row < 10 else ((2, row - 10) if row < 18 else (3, row - 18)))
        for parity in range(2):
            for ch in range(3):
                perm[parity * 128 + row * 6 + parity * 3 + ch, region * 24 + ch * 8 + inner] = 1
    pick = np.zeros((2, 64, 128), np.float32)
    for parity in range(2):
        for pair in range(64):
            pick[parity, pair, 2 * pair + parity] = 1
    return perm, pick


def slot_of(ry, rx):
    return (rx // 2) * 8 + ry * 2 + rx % 2


def weight_table():
    table = np.zeros((84, 16 * 256), np.float32)
    for ry in range(4):
        for rx in range(4):
            base = slot_of(ry, rx) * 256
            for ky in range(3):
                for kx in range(3):
                    for kt in range(3):
                        for ch in range(3):
                            row, col = ry + ky, rx + kx
                            lane = (col // 2 - rx // 2) * 36 + row * 6 + (col % 2) * 3 + ch
                            table[(ky * 9 + kt * 3 + ch) * 3 + kx, base + kt * 72 + lane] = 1
            for part in range(3):
                table[81 + part, base + 216 + part] = 1
    return table


def clip_age(starts, t):
    latest = jnp.zeros_like(t)
    for i in range(1, 6):
        latest = jnp.where(starts[i] <= t, starts[i], latest)
    return t - latest


def clip_starts(clip_s):
    starts = [jnp.int32(0)]
    for i in range(5):
        starts.append(starts[-1] + clip_s[i])
    return starts


PLAN = 1024


def plan_steps(tok, total, base, first, last):
    sub = lax.broadcasted_iota(jnp.int32, (32, PLAN), 0)
    high_of = ((sub % 8) * 4 + sub // 8).astype(F32).astype(BF)
    low_of = sub.astype(F32).astype(BF)
    lane = lax.broadcasted_iota(jnp.int32, (32, PLAN), 1)
    inside = (lane % 256).astype(F32).astype(BF)
    frame = (lane // 256).astype(F32)
    none = jnp.zeros((32, PLAN), BF)
    ones = jnp.ones((32, PLAN), BF)

    def spread_rows(rows):
        wide = [jnp.broadcast_to(rows[i : i + 1], (32, 128)).astype(BF) for i in range(8)]
        return jnp.concatenate(wide, axis=1)

    def step(q, carry):
        rows = tok[pl.ds(pl.multiple_of(q * 8, 8), 8), :] - base
        high = spread_rows(jnp.clip(rows >> 5, -1, 64).astype(F32))
        low = spread_rows((rows & 31).astype(F32))
        hit = high == high_of
        times = jnp.where(hit, (frame + (q * (PLAN // 256)).astype(F32)).astype(BF), none)
        left = jnp.concatenate([times, jnp.where(hit, inside, none)], axis=0)
        right = jnp.where(low == low_of, ones, none)
        total[...] += lax.dot_general(left, right, NT, preferred_element_type=F32)
        return carry

    lax.fori_loop(first, last, step, 0, unroll=4)


def plan_words(total, starts, words, entry):
    found = (total[:32, :] * 256.0 + total[32:, :]).astype(jnp.int32)
    e = jnp.concatenate([found[8 * m : 8 * m + 8] for m in range(4)], axis=1)
    entry[...] = e
    t, j, col = e >> 8, (e >> 6) & 3, e & 63
    words[0:8, :] = t * FRAME_ROWS + 7 + col
    words[8:16, :] = j
    words[16:24, :] = 4 - clip_age(starts, t)


def lay_second(weight, w2, kt, dy, dx):
    zero = jnp.zeros((CH, CH), F32)
    blocks = []
    for ry in range(4):
        for rx in range(4):
            ky, kx = ry - dy, rx - dx
            within = 0 <= ky < 3 and 0 <= kx < 3
            blocks.append(weight[ky, kx, :, kt * CH : (kt + 1) * CH].astype(F32) if within else zero)
    row = (dy * 2 + dx) * CH
    w2[kt, row : row + CH, :] = jnp.concatenate(blocks, axis=1).astype(BF)


def gather_taps(in_weight, in_bias, taps):
    rest = in_bias[...]
    split = []
    for _ in range(3):
        part = rest.astype(BF).astype(F32)
        split.append(part)
        rest = rest - part
    rows = [in_weight[ky, i].astype(F32) for ky in range(3) for i in range(9)]
    taps[...] = jnp.transpose(jnp.concatenate(rows + split, axis=0)).astype(BF)


def lay_first(taps, spread, w1, ry):
    for pos in range(4 * ry, 4 * ry + 4):
        w1[pos * CH : (pos + 1) * CH, :] = lax.dot_general(
            taps[...], spread[:, pos * 256 : (pos + 1) * 256], NN, preferred_element_type=F32
        ).astype(BF)


SUBS = 2
PLAN_A = 64
LAG = 12
PACE = 1


def gather_kernel(
    clip_hbm,
    slab_hbm,
    pix,
    tok_hbm,
    perm_hbm,
    pick_hbm,
    spread_hbm,
    in_weight_hbm,
    in_bias_hbm,
    gain_hbm,
    weight_hbm,
    bias_hbm,
    out,
    words,
    entry,
    scales,
    w1,
    w2,
    clip_s,
    slab,
    mine_v,
    tok,
    perm,
    pick,
    spread,
    in_weight,
    in_bias,
    gain,
    weight,
    bias,
    load_sem,
    taps,
    own,
    edge,
    total,
    s0,
    r0,
    s1,
    r1,
    keep,
    s2,
    r2,
    s3,
    r3,
    s4,
    r4,
):
    w = lax.axis_index("wide")
    n = lax.axis_index("narrow")
    z, y = w // RING, w % RING
    x, c = n // 2, n % 2
    sibling = (w, x * 2 + 1 - c)
    near = x + 2 * c - 1
    near_ok = jnp.logical_and(near >= 0, near <= 3)
    major = (z, y)
    minor = (y, z)

    def wide_of(piece, maj, mnr):
        return maj * RING + mnr if piece == 0 else mnr * RING + maj

    def along_minor(piece, d):
        return (wide_of(piece, major[piece], (minor[piece] + d) % RING), n)

    def along_major(piece, d):
        return (wide_of(piece, (major[piece] + d) % RING, minor[piece]), n)

    pairs = [
        (pix.at[pl.ds(2 * c, 2)], mine_v),
        (perm_hbm, perm),
        (pick_hbm, pick),
        (tok_hbm, tok),
        (spread_hbm, spread),
        (in_weight_hbm, in_weight),
        (in_bias_hbm, in_bias),
        (weight_hbm, weight),
        (clip_hbm, clip_s),
        (slab_hbm, slab),
        (gain_hbm, gain),
        (bias_hbm, bias),
    ]
    loads = [pltpu.make_async_copy(src, dst, load_sem.at[i]) for i, (src, dst) in enumerate(pairs)]
    for copy in loads:
        copy.start()

    barrier = pltpu.get_barrier_semaphore()
    pl.semaphore_signal(barrier, inc=1, device_id=sibling, device_id_type=MESH)
    for piece in range(2):
        for d in range(1, RING):
            pl.semaphore_signal(barrier, inc=1, device_id=along_minor(piece, d), device_id_type=MESH)

    for side in (1, 3):
        for core in range(2):
            beside = ((x + side) % 4) * 2 + core
            pl.semaphore_signal(barrier, inc=1, device_id=(w, beside), device_id_type=MESH)
    pl.semaphore_wait(barrier, 19)

    def to_sibling():
        return pltpu.make_async_remote_copy(
            pix.at[pl.ds(2 * (1 - c), 2)], edge.at[0], s0.at[0], r0.at[0], sibling, MESH
        )

    def to_near(core):
        return pltpu.make_async_remote_copy(
            pix.at[pl.ds(2 * core, 2)],
            edge.at[2 - c],
            s0.at[1 + core],
            r0.at[2 - c],
            (w, jnp.clip(near, 0, 3) * 2 + core),
            MESH,
        )

    def arrival(region):
        return pltpu.make_async_remote_copy(
            pix.at[pl.ds(0, 2)], edge.at[region], s0.at[0], r0.at[region], sibling, MESH
        )

    to_sibling().start()

    @pl.when(near_ok)
    def _():
        to_near(0).start()
        to_near(1).start()

    @pl.when(x == 0)
    def _():
        edge[1] = jnp.zeros_like(edge[1])

    @pl.when(x == 3)
    def _():
        edge[2] = jnp.zeros_like(edge[2])

    arrival(0).wait_recv()

    @pl.when(x > 0)
    def _():
        arrival(1).wait_recv()

    @pl.when(x < 3)
    def _():
        arrival(2).wait_recv()

    for copy in loads[:3]:
        copy.wait()
    for piece in range(2):
        mine = mine_v[piece].astype(F32).reshape(24, 128)
        other = edge[0, piece].astype(F32).reshape(24, 128)
        low = edge[1, piece].astype(F32).reshape(24, 128)
        high = edge[2, piece].astype(F32).reshape(24, 128)
        first = jnp.where(c == 0, mine, other)
        second = jnp.where(c == 0, other, mine)
        stack = jnp.concatenate([low, first, second, high], axis=0).astype(BF)
        laid = lax.dot_general(perm[...], stack, NN, preferred_element_type=F32).astype(BF)
        rows = lax.dot_general(pick[0], laid[:128], NT, preferred_element_type=F32)
        rows += lax.dot_general(pick[1], laid[128:], NT, preferred_element_type=F32)
        own[piece] = rows.astype(BF)

    def local(piece):
        return pltpu.make_async_copy(own.at[piece], out.at[piece, c, major[piece], minor[piece]], keep.at[piece])

    def first_hop(piece, d, slot):
        return pltpu.make_async_remote_copy(
            own.at[piece],
            out.at[piece, c, major[piece], slot],
            s1.at[piece, d],
            r1.at[piece, d],
            along_minor(piece, d),
            MESH,
        )

    order = (4, 3, 5, 2, 6, 1, 7)
    for piece in range(2):
        for d in order:
            first_hop(piece, d, minor[piece]).start()
    for piece in range(2):
        local(piece).start()

    for copy in loads[3:]:
        copy.wait()
    total[...] = jnp.zeros_like(total)
    plan_steps(tok, total, w * TOK, 0, PLAN_A)

    def last_words():
        plan_words(total, clip_starts(clip_s), words, entry)
        words[24:26, :] = slab[...]
        scales[0:1, 0:CH] = gain[...]
        scales[1:2, 0:CH] = bias[...]

    work = [
        functools.partial(plan_steps, tok, total, w * TOK, q, q + 8) for q in range(PLAN_A, TOK * 64 // PLAN, 8)
    ]
    work += [functools.partial(gather_taps, in_weight, in_bias, taps), last_words]
    work += [functools.partial(lay_first, taps, spread, w1, ry) for ry in range(4)]
    work += [
        functools.partial(lay_second, weight, w2, kt, dy, dx)
        for kt in range(3)
        for dy in range(2)
        for dx in range(2)
    ]

    part = RING // SUBS

    def hop(piece, way, k, h, arrived):
        step = 1 - 2 * way
        chunk = (major[piece] - step * (k if arrived else k - 1)) % RING
        ref = out.at[piece, c, chunk, pl.ds(part * h, part)]
        return pltpu.make_async_remote_copy(
            ref, ref, s2.at[piece, way, k - 1, h], r2.at[piece, way, k - 1, h], along_major(piece, step), MESH
        )

    def share(piece, way, k, h, core):
        chunk = (major[piece] - (1 - 2 * way) * k) % RING
        where = (piece, core, chunk, pl.ds(part * h, part))
        return pltpu.make_async_remote_copy(
            out.at[where], out.at[where], s3.at[piece, way, k - 1, h], r3.at[piece, way, k - 1, h], sibling, MESH
        )

    def share_own(piece, core):
        where = (piece, core, major[piece])
        return pltpu.make_async_remote_copy(out.at[where], out.at[where], s4.at[piece], r4.at[piece], sibling, MESH)

    def turned(way, i):
        return i if way == 0 else SUBS - 1 - i

    for piece in range(2):
        local(piece).wait()
        for d in reversed(order):
            first_hop(piece, d, (minor[piece] - d) % RING).wait_recv()
        for i in range(SUBS):
            for way in range(2):
                hop(piece, way, 1, turned(way, i), False).start()
    for piece in range(2):
        share_own(piece, c).start()

    moves = []
    for k in range(1, 5):
        for i in range(SUBS):
            for piece in range(2):
                for way in range(2):
                    if k < 4 or i < SUBS // 2:
                        moves.append((piece, way, k, turned(way, i), k < 3 or (k == 3 and i < SUBS // 2)))
    to_sibling().wait_send()

    @pl.when(near_ok)
    def _():
        to_near(0).wait_send()
        to_near(1).wait_send()

    for at, (piece, way, k, h, onward) in enumerate(moves):
        hop(piece, way, k, h, True).wait_recv()
        if onward:
            hop(piece, way, k + 1, h, False).start()
        share(piece, way, k, h, c).start()
        if at < 14:
            first_hop(at % 2, order[at // 2], minor[at % 2]).wait_send()
        if at >= LAG:
            hop(*moves[at - LAG][:4], False).wait_send()
            share(*moves[at - LAG][:4], c).wait_send()
        for _ in range(PACE):
            if work:
                work.pop(0)()
    for task in work:
        task()

    for piece in range(2):
        share_own(piece, c).wait_send()
        share_own(piece, 1 - c).wait_recv()
    for at, (piece, way, k, h, onward) in enumerate(moves):
        if at >= len(moves) - LAG:
            hop(piece, way, k, h, False).wait_send()
            share(piece, way, k, h, c).wait_send()
        share(piece, way, k, h, 1 - c).wait_recv()


def gather_tables(clip_lengths, slab_place, pixel_slabs, tok_place, in_weight, in_bias, gain, weight, bias):
    perm, pick = placement_tables()
    dma = pltpu.SemaphoreType.DMA
    vmem = pl.BlockSpec(memory_space=pltpu.VMEM)
    shape = (2, 2, RING, RING, 64, 128)
    return pl.pallas_call(
        gather_kernel,
        out_shape=(
            jax.ShapeDtypeStruct(shape, BF),
            jax.ShapeDtypeStruct((32, 128), jnp.int32),
            jax.ShapeDtypeStruct((8, 128), jnp.int32),
            jax.ShapeDtypeStruct((8, 128), F32),
            jax.ShapeDtypeStruct((16 * CH, 256), BF),
            jax.ShapeDtypeStruct((3, 4 * CH, 16 * CH), BF),
        ),
        in_specs=[pl.BlockSpec(memory_space=pltpu.HBM)] * 12,
        out_specs=(pl.BlockSpec(memory_space=pl.ANY), vmem, vmem, vmem, vmem, vmem),
        scratch_shapes=[
            pltpu.SMEM((6,), jnp.int32),
            pltpu.VMEM((2, 128), jnp.int32),
            pltpu.VMEM((2, 3, 8, 128), BF),
            pltpu.VMEM((512, 128), jnp.int32),
            pltpu.VMEM((256, 96), BF),
            pltpu.VMEM((2, 64, 128), BF),
            pltpu.VMEM((84, 16 * 256), BF),
            pltpu.VMEM((3, 9, 3, CH), BF),
            pltpu.VMEM((1, CH), F32),
            pltpu.VMEM((1, CH), F32),
            pltpu.VMEM((3, 3, CH, 3 * CH), BF),
            pltpu.VMEM((1, CH), F32),
            dma((12,)),
            pltpu.VMEM((CH, 84), BF),
            pltpu.VMEM((2, 64, 128), BF),
            pltpu.VMEM((3, 2, 3, 8, 128), BF),
            pltpu.VMEM((64, 32), F32),
            dma((3,)),
            dma((3,)),
            dma((2, RING)),
            dma((2, RING)),
            dma((2,)),
            dma((2, 2, 4, SUBS)),
            dma((2, 2, 4, SUBS)),
            dma((2, 2, 4, SUBS)),
            dma((2, 2, 4, SUBS)),
            dma((2,)),
            dma((2,)),
        ],
        compiler_params=pltpu.CompilerParams(
            collective_id=0, has_side_effects=True, vmem_limit_bytes=16 << 20
        ),
        name="gather_tables",
    )(
        *[pltpu.with_memory_space_constraint(v, pltpu.HBM) for v in (
        clip_lengths,
        slab_place.reshape(2, 128),
        pixel_slabs,
        tok_place.reshape(512, 128),
        jnp.asarray(perm, BF),
        jnp.asarray(pick, BF),
        jnp.asarray(weight_table(), BF),
        jnp.transpose(in_weight, (0, 3, 1, 2)),
        in_bias.reshape(1, CH),
        gain.reshape(1, CH),
        weight,
        bias.reshape(1, CH),
        )]
    )


TILE = 1024
BATCH = 32


def column(row):
    n = row.shape[1]
    same = lax.broadcasted_iota(jnp.int32, (n, n), 0) == lax.broadcasted_iota(jnp.int32, (n, n), 1)
    return jnp.sum(jnp.where(same, jnp.broadcast_to(row, (n, n)), 0.0), axis=1, keepdims=True)


def main_kernel(
    words_any, entry, least, table, scales, w1, w2, out, frames, patches, shifts, hid, act, words, words_sem
):
    fetch = pltpu.make_async_copy(words_any, words, words_sem)
    fetch.start()
    n = lax.axis_index("narrow")
    c = n % 2

    half_gain = column(scales[0:1, 0:CH]) * 0.5
    out_bias = column(scales[1:2, 0:CH])
    lane = lax.broadcasted_iota(jnp.int32, (8, 128), 1)
    for j in range(4):
        shifts[8 * j : 8 * j + 8, :] = (lane + 256 - (48 * c + 12 * j)) & 127

    frames[0 : LEAD * FRAME_ROWS, :] = jnp.zeros((LEAD * FRAME_ROWS, 128), F32)
    frames[(LEAD + 256) * FRAME_ROWS : (LEAD + 256) * FRAME_ROWS + 8, :] = jnp.zeros((8, 128), F32)
    fetch.wait()
    for k in range(8):
        piece, core = k // 4, (k // 2) % 2

        def fill(m, carry):
            maj = (k % 2) * 4 + m
            at = []
            for mnr in range(RING):
                wide = maj * RING + mnr if piece == 0 else mnr * RING + maj
                frame = words[3 * TOK + wide * 4 + core * 2 + piece]
                at.append(pl.multiple_of((frame + LEAD) * FRAME_ROWS, 8))
            for mnr in range(RING):
                frames[pl.ds(at[mnr], 8), :] = jnp.zeros((8, 128), F32)
                frames[pl.ds(at[mnr] + 8, 64), :] = table[32 * k + m * RING + mnr].astype(F32)
            return carry

        lax.fori_loop(0, 4, fill, 0)

    late = lax.broadcasted_iota(jnp.int32, (5, 128), 0)

    def pick_up(s):
        base, j, oldest = words[s], words[TOK + s], words[2 * TOK + s]
        rel = shifts[pl.ds(pl.multiple_of(j * 8, 8), 5), :]
        left = frames[pl.ds(base, 5, stride=FRAME_ROWS), :]
        mid = pltpu.roll(frames[pl.ds(base + 1, 5, stride=FRAME_ROWS), :], 36, 1)
        right = pltpu.roll(frames[pl.ds(base + 2, 5, stride=FRAME_ROWS), :], 72, 1)
        row = jnp.where(rel < 36, left, jnp.where(rel < 72, mid, jnp.where(rel < 108, right, 1.0)))
        row = jnp.where(late >= oldest, row, 0.0)
        return pltpu.roll(row, (256 - 48 * c - 12 * j) & 127, 1)

    def pull(q, carry):
        rows = [pick_up(q * BATCH + i) for i in range(BATCH)]
        for i in range(BATCH):
            patches[pl.ds(q * BATCH + i, 5, stride=TOK), :] = rows[i]
        return carry

    lax.fori_loop(0, TOK // BATCH, pull, 0)

    def tile(g, carry):
        at = pl.multiple_of(g * TILE, TILE)
        e, old = [
            jnp.concatenate([ref[pl.ds(g * (TILE // 128) + i, 1), :] for i in range(TILE // 128)], axis=1)
            for ref in (entry, least.at[pl.ds(16, 8)])
        ]
        j, col, age = (e >> 6) & 3, e & 63, 4 - old
        row_ok = [
            jnp.logical_not(jnp.logical_and(j == 0, n == 0)),
            None,
            None,
            jnp.logical_not(jnp.logical_and(j == 3, n == 7)),
        ]
        col_ok = [col != 0, None, None, col != 63]
        spot = lax.broadcasted_iota(jnp.int32, (TILE, 128), 1)
        total = jnp.concatenate([jnp.broadcast_to(out_bias, (CH, TILE))] * 4, axis=0)
        for s in range(3):
            seen = [patches[pl.ds(pl.multiple_of((s + kt) * TOK + at, TILE), TILE), :] for kt in range(3)]
            for half in range(2):
                start = seen[0] if half == 0 else pltpu.roll(seen[0], 92, 1)
                middle = pltpu.roll(seen[1], 72 - 36 * half, 1)
                end = pltpu.roll(seen[2], 16 if half == 0 else 108, 1)
                left = jnp.where(spot < 72, start, middle).astype(BF)
                right = jnp.where(spot < 16, middle, jnp.where(spot < 88, end, 1.0)).astype(BF)
                rows = slice(half * 8 * CH, (half + 1) * 8 * CH)
                hid[rows, :] = lax.dot_general(
                    w1[rows, :], jnp.concatenate([left, right], axis=1), NT, preferred_element_type=F32
                )
            for ry in range(4):
                for rx in range(4):
                    pos = ry * 4 + rx
                    slot = slot_of(ry, rx) * CH
                    h = hid[slot : slot + CH, :]
                    scale = lax.rsqrt(jnp.sum(h * h, axis=0, keepdims=True) * (1.0 / CH) + EPSILON)
                    ok = age >= 2 - s
                    if row_ok[ry] is not None:
                        ok = jnp.logical_and(ok, row_ok[ry])
                    if col_ok[rx] is not None:
                        ok = jnp.logical_and(ok, col_ok[rx])
                    u = h * jnp.where(ok, scale, 0.0) * half_gain
                    act[pos * CH : (pos + 1) * CH, :] = (u + u * jnp.tanh(u)).astype(BF)
            total = total + lax.dot_general(w2[s], act[...], NN, preferred_element_type=F32)
            if s == 2:
                keep = [hid[slot_of(ry, rx) * CH : slot_of(ry, rx) * CH + CH, :] for ry in (1, 2) for rx in (1, 2)]
                total = total + jnp.concatenate(keep, axis=0)
        out[pl.ds(at, TILE), :] = jnp.transpose(total).astype(BF)
        return carry

    lax.fori_loop(0, TOK // TILE, tile, 0)


def encode(words, entry, table, scales, w1, w2):
    vmem = pl.BlockSpec(memory_space=pltpu.VMEM)
    return pl.pallas_call(
        main_kernel,
        out_shape=jax.ShapeDtypeStruct((TOK, 4 * CH), BF),
        in_specs=[pl.BlockSpec(memory_space=pl.ANY)] + [vmem] * 6,
        out_specs=vmem,
        scratch_shapes=[
            pltpu.VMEM(((LEAD + 256) * FRAME_ROWS + 8, 128), F32),
            pltpu.VMEM((5 * TOK, 128), F32),
            pltpu.VMEM((32, 128), jnp.int32),
            pltpu.VMEM((16 * CH, TILE), F32),
            pltpu.VMEM((16 * CH, TILE), BF),
            pltpu.SMEM((4 * TOK,), jnp.int32),
            pltpu.SemaphoreType.DMA,
        ],
        compiler_params=pltpu.CompilerParams(vmem_limit_bytes=42 << 20),
        name="encode",
    )(words.reshape(4 * TOK), entry, words, table.reshape(256, 64, 128), scales, w1, w2)


def body(
    pixel_slabs,
    conv_in_weight,
    conv_in_bias,
    norm_gain,
    conv_weight,
    conv_bias,
    clip_lengths,
    slab_place,
    tok_place,
):
    table, words, entry, scales, w1, w2 = gather_tables(
        clip_lengths,
        slab_place,
        pixel_slabs,
        tok_place,
        conv_in_weight,
        conv_in_bias,
        norm_gain,
        conv_weight,
        conv_bias,
    )
    return encode(words, entry, table, scales, w1, w2)


def solution(mesh):
    placed = (P("wide", None, "narrow", None), P(), P(), P(), P(), P(), P(), P(), P())
    return jax.shard_map(
        body, mesh=mesh, in_specs=placed, out_specs=P(("wide", "narrow"), None), check_vma=False
    )
```
